1024 devices in a mesh: dp: 16 (over x, core), mp: 8 (over z), rep: 8 (over y).
Axes of the slice: x: 8, y: 8, z: 8, core: 2. Of those that a mesh axis runs over, the one named last changes fastest.
Arguments:
- query_rows: bfloat16 [16384, 1280], P(('dp', 'mp', 'rep')), may hold values from -64 to 64
- key_rows: bfloat16 [16384, 1280], P(('dp', 'mp', 'rep')), may hold values from -7 to 7
- value_rows: bfloat16 [16384, 1280], P(('dp', 'mp', 'rep')), may hold values from -6 to 6
- residual: bfloat16 [16384, 1280], P(('dp', 'mp', 'rep')), may hold values from -6 to 6
- out_proj: bfloat16 [1280, 1280], replicated, may hold values from -0.15625 to 0.15625
- merge_gain: float32 [1280], replicated, may hold values from 0.1 to 1.9
- merger_proj: bfloat16 [5120, 8192], P(None, ('mp', 'rep')), may hold values from -1.5 to 1.5
- model_gain: float32 [8192], P(('mp', 'rep')), may hold values from 0.1 to 1.9
- image_grid: int32 [1024, 2], replicated, may hold values from 1 to 4, as said below
- image_group: int32 [1024], replicated, may hold values from 0 to 15, as said below
- rollout_image: int32 [16384], P('dp'), may hold values from 0 to 1023, as said below
- cotangent: bfloat16 [65536, 8192], P('dp', ('mp', 'rep')), may hold values from -0.078125 to 0.078125
Outputs:
- normed_tokens: bfloat16 [4096, 8192], P('dp', ('mp', 'rep'))
- merger_grad: float32 [5120, 8192], P('dp', ('mp', 'rep'))
The draws below stay inside these ranges and needn't reach their ends.
Inputs may be any that keep to these rules, and one draw needn't show every extreme that they name: `image_grid`: height times width of every image is between 1 and 4; image 0 has height 4 and width 1. `image_group`: every rollout group receives exactly 64 images. Among the 64 images of one owner group (images k * 64 to k * 64 + 63) at most 5 go to any one rollout group, and every owner group sends exactly 5 to some rollout group. `rollout_image`: rollouts come in blocks of 1024, one block a rollout group in order of group; every image has exactly 16 rollouts, all in the block of its image_group.
All inputs are finite; a program needn't handle non-finite values.
Results may differ from the reference program's by a relative error of at most 0.02.
Values may be sent and summed in bfloat16 or wider, within the bound.
A program may use at most 64 MiB of HBM per device.

```python
import jax
import jax.numpy as jnp
import numpy as np
from jax import lax

DV = 1280
HEADS = 16
D = 8192
IMG_TOK = 4
ROLL = 16
HEAD = 80
DM = 5120
PATCH_SLOTS = 16
IMAGES = 1024
GROUPS = 16
IMGS_G = 64
CAP = 5
ROLLOUTS = 16384
PATCHES = 16384


def routing_plan(key):
    per_shift = np.clip(IMGS_G - np.arange(GROUPS) * CAP, 0, CAP)
    shift_list = np.repeat(np.arange(GROUPS), per_shift).astype(np.int32)
    shifts = jax.random.permutation(jax.random.fold_in(key, 71), jnp.asarray(shift_list, dtype=jnp.int32))
    labels = jax.random.permutation(jax.random.fold_in(key, 72), GROUPS).astype(jnp.int32)
    owners = jnp.arange(GROUPS, dtype=jnp.int32)[:, None]
    destination = labels[(owners + shifts[None, :]) % GROUPS].reshape(-1).astype(jnp.int32)
    image_order = jnp.argsort(destination, stable=True).astype(jnp.int32).reshape(GROUPS, IMGS_G)
    repeated = jnp.repeat(image_order, ROLL, axis=1)
    width_all = IMGS_G * ROLL
    scores = jax.random.randint(jax.random.fold_in(key, 73), (GROUPS, width_all), 0, 65536, dtype=jnp.int32)
    scores = scores * width_all + jnp.arange(width_all, dtype=jnp.int32)[None, :]
    shuffle = jnp.argsort(scores, axis=1)
    rollouts = jnp.take_along_axis(repeated, shuffle, axis=1).reshape(-1).astype(jnp.int32)
    return (destination, rollouts)


def draw_image_group(key, part):
    return routing_plan(key)[0]


def draw_rollout_image(key, part):
    return routing_plan(key)[1]


def draw_image_grid(key, part):
    wide_seed, tall_seed = jax.random.split(jax.random.fold_in(key, 81))
    grid_wide = jnp.minimum(jax.random.randint(wide_seed, (IMAGES,), 1, 3, dtype=jnp.int32), IMG_TOK)
    highest = IMG_TOK // grid_wide
    grid_tall = 1 + jax.random.randint(tall_seed, (IMAGES,), 0, 1 << 20, dtype=jnp.int32) % highest
    grid_wide = grid_wide.at[0].set(1)
    grid_tall = grid_tall.at[0].set(IMG_TOK)
    return jnp.stack([grid_tall, grid_wide], axis=1).astype(jnp.int32)


def attention_pair(key):
    query_seed, key_seed = jax.random.split(jax.random.fold_in(key, 91))
    queries = jax.random.truncated_normal(query_seed, -6.0, 6.0, (PATCHES, DV), jnp.float32)
    keys_all = jax.random.truncated_normal(key_seed, -6.0, 6.0, (PATCHES, DV), jnp.float32)
    return (queries, keys_all)


def draw_query_rows(key, part):
    return attention_pair(key)[0].astype(jnp.bfloat16)


def draw_key_rows(key, part):
    return attention_pair(key)[1].astype(jnp.bfloat16)


def draw_merger_proj(key, part):
    weight_seed, column_seed = jax.random.split(jax.random.fold_in(key, 101))
    column = jnp.arange(D, dtype=jnp.float32) / D
    jitter = jax.random.truncated_normal(column_seed, -2.0, 2.0, (D,), jnp.float32)
    ramp = 10.0 ** column * jnp.exp(0.25 * jitter) / 4.64
    values_all = jax.random.truncated_normal(weight_seed, -6.0, 6.0, (DM, D), jnp.float32)
    return (values_all * ramp[None, :] * DM ** (-0.5)).astype(jnp.bfloat16)


def steps_of(own_key, extent, pieces, smallest, largest):
    level, own = 1.0, jax.random.fold_in(own_key, 6)
    for dim, shards_of in pieces:
        draws = jnp.exp(jax.random.uniform(jax.random.fold_in(own, dim), (shards_of,), jnp.float32, smallest / len(pieces), largest / len(pieces)))
        level = level * jnp.repeat(draws, extent[dim] // shards_of).reshape([-1 if axis == dim else 1 for axis in range(len(extent))])
    return level


def bell_draw(key, dims, width, limit, cuts=(), kind=jnp.bfloat16):
    factor_of = steps_of(key, dims, cuts, -0.22, 0.18) if cuts else 1.0
    result = jax.random.normal(key, dims, jnp.float32) * width * factor_of
    return jnp.minimum(jnp.maximum(result, -limit), limit).astype(kind)


def setup_inputs(seed: int = 0) -> dict:
    key_of = jax.random.split(jax.random.key(seed), 13)
    query_rows = draw_query_rows(jax.random.fold_in(key_of[12], 71), 0)
    key_rows = draw_key_rows(jax.random.fold_in(key_of[12], 71), 0)
    value_rows = bell_draw(key_of[2], (PATCHES, DV), 1.0, 6.0, ((0, 1024),))
    residual = bell_draw(key_of[3], (PATCHES, DV), 1.0, 6.0, ((0, 1024),))
    out_proj = bell_draw(key_of[4], (DV, DV), DV ** -0.5, 0.15625)
    merge_gain = jnp.clip(1.0 + 0.18 * jax.random.normal(key_of[5], (DV,), jnp.float32), 0.1, 1.9)
    merger_proj = draw_merger_proj(jax.random.fold_in(key_of[12], 71), 0)
    model_gain = jnp.clip(1.0 + 0.18 * jax.random.normal(key_of[7], (D,), jnp.float32), 0.1, 1.9)
    image_grid = draw_image_grid(jax.random.fold_in(key_of[12], 71), 0)
    image_group = draw_image_group(jax.random.fold_in(key_of[12], 71), 0)
    rollout_image = draw_rollout_image(jax.random.fold_in(key_of[12], 71), 0)
    cotangent = bell_draw(key_of[11], (ROLLOUTS * IMG_TOK, D), 0.005, 0.078125, ((0, 16), (1, 64)))
    return dict(query_rows=query_rows, key_rows=key_rows, value_rows=value_rows, residual=residual, out_proj=out_proj, merge_gain=merge_gain, merger_proj=merger_proj, model_gain=model_gain, image_grid=image_grid, image_group=image_group, rollout_image=rollout_image, cotangent=cotangent)


EPSILON = 1e-06

def reference(query_rows, key_rows, value_rows, residual, out_proj, merge_gain, merger_proj, model_gain, image_grid, image_group, rollout_image, cotangent):
    counts = (image_grid[:, 0] * image_grid[:, 1]).astype(jnp.int32)
    patch_valid = jnp.arange(PATCH_SLOTS, dtype=jnp.int32)[None, :] < 4 * counts[:, None]
    query_heads = query_rows.astype(jnp.float32).reshape(IMAGES, PATCH_SLOTS, HEADS, HEAD)
    key_heads = key_rows.astype(jnp.float32).reshape(IMAGES, PATCH_SLOTS, HEADS, HEAD)
    value_heads = value_rows.astype(jnp.float32).reshape(IMAGES, PATCH_SLOTS, HEADS, HEAD)
    scores = jnp.einsum('iphd,ikhd->ihpk', query_heads, key_heads) * HEAD ** (-0.5)
    scores = jnp.where(patch_valid[:, None, None, :], scores, -1e+30)
    attn_weights = jax.nn.softmax(scores, axis=-1).astype(jnp.bfloat16)
    attended = jnp.einsum('ihpk,ikhd->iphd', attn_weights.astype(jnp.float32), value_heads)
    attended = attended.astype(jnp.bfloat16).reshape(IMAGES * PATCH_SLOTS, DV)
    mixed_rows = residual.astype(jnp.float32) + jnp.dot(attended, out_proj, preferred_element_type=jnp.float32)
    inverse_rms = lax.rsqrt(lax.optimization_barrier(jnp.mean(mixed_rows * mixed_rows, axis=-1, keepdims=True)) + EPSILON)
    valid_rows = patch_valid.reshape(-1, 1).astype(jnp.float32)
    merged = (mixed_rows * inverse_rms * merge_gain * valid_rows).astype(jnp.bfloat16).reshape(IMAGES * IMG_TOK, DM)
    projected = jnp.dot(merged, merger_proj, preferred_element_type=jnp.float32).astype(jnp.bfloat16)
    image_order = jnp.argsort(image_group, stable=True).astype(jnp.int32)
    model_input = projected.reshape(IMAGES, IMG_TOK, D)[image_order]
    hidden = model_input.astype(jnp.float32)
    inverse = lax.rsqrt(lax.optimization_barrier(jnp.sum(hidden * hidden, axis=-1)) / D + EPSILON)
    normed_tokens = (hidden * inverse[..., None] * model_gain).astype(jnp.bfloat16).reshape(IMAGES * IMG_TOK, D)
    position = jnp.argsort(image_order).astype(jnp.int32)
    rollout_pos = position[rollout_image].reshape(GROUPS, IMGS_G * ROLL)
    rollout_pos = rollout_pos - (jnp.arange(GROUPS, dtype=jnp.int32) * IMGS_G)[:, None]
    grouped_cot = cotangent.reshape(GROUPS, IMGS_G * ROLL, IMG_TOK * D)

    def group_sum(packed):
        local_pos, cot_block = packed
        return jax.ops.segment_sum(cot_block.astype(jnp.float32), local_pos, num_segments=IMGS_G)
    summed = lax.map(group_sum, (rollout_pos, grouped_cot)).reshape(IMAGES, IMG_TOK, D)
    token_valid = jnp.arange(IMG_TOK, dtype=jnp.int32)[None, :] < counts[image_order][:, None]
    summed = summed * token_valid[..., None].astype(jnp.float32)
    inner_sum = lax.optimization_barrier(jnp.sum(summed * model_gain * hidden, axis=-1))
    token_grad = inverse[..., None] * model_gain * summed - hidden * (inverse ** 3 / D * inner_sum)[..., None]
    token_grad = token_grad.astype(jnp.bfloat16).reshape(IMAGES * IMG_TOK, D)
    merged_sorted = merged.reshape(IMAGES, IMG_TOK, DM)[image_order].reshape(IMAGES * IMG_TOK, DM)
    merger_grad = jnp.dot(merged_sorted.T, token_grad, preferred_element_type=jnp.float32)
    return (normed_tokens, merger_grad)
```

```python
import functools

import jax
import jax.numpy as jnp
from jax import lax
from jax.experimental import pallas as pl
from jax.experimental.pallas import tpu as pltpu
from jax.sharding import PartitionSpec as P

HEADS = 16
HEAD = 80
DV = 1280
D = 8192
EPSILON = 1e-06
RING = 8
GROUPS = 16
MEMBERS = 64
SLOTS = 16
ROWS = MEMBERS * SLOTS
TOKENS = MEMBERS * 4
HALF = DV // 2
COLS = 128
BLOCK = 32
ROUTED = GROUPS * BLOCK
PIECE = 320
MESH = pl.DeviceIdType.MESH
F32 = jnp.float32
BF16 = jnp.bfloat16


def iota(shape, dim):
    return lax.broadcasted_iota(jnp.int32, shape, dim)


def dot(a, b):
    return jnp.dot(a, b, preferred_element_type=F32)


def dot_first(a, b):
    return lax.dot_general(a, b, (((0,), (0,)), ((), ())), preferred_element_type=F32)


def remote(src, dst, send, recv, device):
    return pltpu.make_async_remote_copy(
        src_ref=src,
        dst_ref=dst,
        send_sem=send,
        recv_sem=recv,
        device_id=device,
        device_id_type=MESH,
    )


def kernel(
    q_hbm,
    k_hbm,
    v_hbm,
    res_hbm,
    wo_hbm,
    merge_gain_ref,
    w_hbm,
    gain_ref,
    grid_ref,
    group_ref,
    roll_ref,
    cot_hbm,
    normed_out,
    grad_out,
    q_buf,
    k_buf,
    v_buf,
    res_buf,
    wo_buf,
    w_buf,
    cot_buf,
    own_buf,
    rows,
    rows_t,
    wide,
    spread,
    row_key,
    pos_key,
    col_key,
    sums,
    sum_out,
    sum_in,
    pick,
    hidden_buf,
    packet,
    z_in,
    y_in,
    norm_out,
    norm_in,
    kept,
    pair_out,
    pair_in,
    chain_out,
    chain_in,
    load_sem,
    gather_send,
    gather_recv,
    sum_send,
    sum_recv,
    stat_send,
    z_recv,
    y_recv,
    norm_send,
    norm_recv,
    pair_send,
    pair_recv,
    chain_send,
    chain_recv,
):
    d = lax.axis_index("dp")
    z = lax.axis_index("mp")
    y = lax.axis_index("rep")
    x = d // 2
    core = d % 2

    loads = [
        pltpu.make_async_copy(q_hbm, q_buf, load_sem.at[0]),
        pltpu.make_async_copy(k_hbm, k_buf, load_sem.at[1]),
        pltpu.make_async_copy(v_hbm, v_buf, load_sem.at[2]),
        pltpu.make_async_copy(res_hbm, res_buf, load_sem.at[3]),
        pltpu.make_async_copy(wo_hbm, wo_buf, load_sem.at[4]),
        pltpu.make_async_copy(cot_hbm, cot_buf, load_sem.at[5]),
    ] + [
        pltpu.make_async_copy(
            w_hbm.at[pl.ds(j * DV, DV), :], w_buf.at[:, pl.ds(j * COLS, COLS)], load_sem.at[6 + j]
        )
        for j in range(4)
    ]
    for load in loads:
        load.start()

    barrier = pltpu.get_barrier_semaphore()

    def greet(axis, me, size):
        def step(i, carry):
            pl.semaphore_signal(
                barrier, inc=1, device_id={axis: (me + i) % size}, device_id_type=MESH
            )
            return carry

        lax.fori_loop(1, size, step, 0)

    greet("mp", z, RING)
    greet("rep", y, RING)
    greet("dp", d, GROUPS)

    factors = grid_ref[...]
    products = factors[0:1, :] * factors[1:2, :]
    counts = jnp.concatenate(
        [products[:, 128 * a : 128 * a + 128] for a in range(8)], axis=0
    ).astype(F32)
    sub8 = iota((8, 128), 0)
    lane8 = iota((8, 128), 1)
    own_image = d * MEMBERS + z * RING + y
    is_own = (sub8 == own_image // 128) & (lane8 == own_image % 128)
    own_count = jnp.sum(
        jnp.sum(jnp.where(is_own, counts, 0.0), axis=0, keepdims=True), axis=1, keepdims=True
    )
    own_valid = own_count * 4.0

    loads[0].wait()
    loads[1].wait()
    head_of_row = iota((256, DV), 0) // SLOTS
    feature = iota((256, DV), 1)
    in_head = (feature >= head_of_row * HEAD) & (feature < head_of_row * HEAD + HEAD)
    queries = jnp.concatenate([q_buf[...].astype(F32)] * HEADS, axis=0)
    queries = jnp.where(in_head, queries, 0.0).astype(BF16)
    scores = lax.dot_general(
        queries, k_buf[...], (((1,), (1,)), ((), ())), preferred_element_type=F32
    ) * HEAD ** (-0.5)
    key_slot = iota((256, SLOTS), 1).astype(F32)
    scores = jnp.where(key_slot < own_valid, scores, -1e30)
    top = jnp.max(scores, axis=1, keepdims=True)
    powers = jnp.exp(scores - top)
    weights = (powers / jnp.sum(powers, axis=1, keepdims=True)).astype(BF16)
    loads[2].wait()
    attended = jnp.where(in_head, dot(weights, v_buf[...]), 0.0)
    attended = jnp.sum(attended.reshape(HEADS, SLOTS, DV), axis=0).astype(BF16)
    loads[3].wait()
    loads[4].wait()
    mixed = res_buf[...].astype(F32) + dot(attended, wo_buf[...])
    inverse_rms = lax.rsqrt(jnp.sum(mixed * mixed, axis=1, keepdims=True) / DV + EPSILON)
    slot_valid = (iota((SLOTS, 1), 0).astype(F32) < own_valid).astype(F32)
    own_buf[...] = (mixed * inverse_rms * merge_gain_ref[...] * slot_valid).astype(BF16)

    def image_rows(zz, yy):
        return pl.ds(pl.multiple_of((zz * RING + yy) * SLOTS, SLOTS), SLOTS)

    def half_of(half, zz, yy):
        return rows.at[image_rows(zz, yy), pl.ds(half * HALF, HALF)]

    pl.semaphore_wait(barrier, 2 * (RING - 1) + GROUPS - 1)

    def push(half, src, zz, yy, device):
        remote(
            src,
            half_of(half, zz, yy),
            gather_send.at[half],
            gather_recv.at[half, zz * RING + yy],
            device,
        ).start()

    def arrive(half, zz, yy):
        ref = half_of(half, zz, yy)
        remote(
            ref,
            ref,
            gather_send.at[half],
            gather_recv.at[half, zz * RING + yy],
            {"rep": (y + 1) % RING},
        ).wait_recv()

    up_y, down_y = {"rep": (y + 1) % RING}, {"rep": (y + RING - 1) % RING}
    up_z, down_z = {"mp": (z + 1) % RING}, {"mp": (z + RING - 1) % RING}
    own0 = own_buf.at[:, pl.ds(0, HALF)]
    own1 = own_buf.at[:, pl.ds(HALF, HALF)]

    def shift(o):
        return (1 - 2 * (o % 2)) * ((o + 1) // 2)

    push(0, own0, z, y, up_y)
    push(0, own0, z, y, down_y)
    push(1, own1, z, y, up_z)
    push(1, own1, z, y, down_z)

    def spread_own(o, carry):
        push(0, own0, z, y, {"mp": (z + RING + shift(o)) % RING})
        push(1, own1, z, y, {"rep": (y + RING + shift(o)) % RING})
        return carry

    lax.fori_loop(1, RING, spread_own, 0)
    rows[image_rows(z, y), :] = own_buf[...]

    groups = group_ref[...]
    arriving = groups == d
    arrived = arriving.astype(F32).astype(BF16)
    before = iota((128, 128), 0)
    after = iota((128, 128), 1)
    earlier = before < after
    rank_in_owner = dot(
        arrived, (earlier & (before // MEMBERS == after // MEMBERS)).astype(F32).astype(BF16)
    )
    rank_in_chunk = dot(arrived, earlier.astype(F32).astype(BF16))
    lower = (iota((8, 8), 0) > iota((8, 8), 1)).astype(F32).astype(BF16)
    chunk_start = jnp.sum(dot(lower, arrived), axis=1, keepdims=True)
    place = rank_in_chunk + chunk_start
    slot_in_chunk = jnp.where(
        arriving, (lane8 // MEMBERS).astype(F32) * 8.0 + rank_in_owner, -1.0
    )
    image_key = (sub8 * 128 + lane8).astype(F32) * 4.0
    slot_of_row = (iota((64, 128), 0) // 4).astype(F32)
    token_of_row = (iota((64, 1), 0) % 4).astype(F32)
    for a in range(8):
        match = slot_in_chunk[a : a + 1, :] == slot_of_row

        def total(value):
            return jnp.sum(jnp.where(match, value[a : a + 1, :], 0.0), axis=1, keepdims=True)

        found = total(counts)
        row_key[64 * a : 64 * a + 64, :] = jnp.where(
            token_of_row < found, total(image_key) + token_of_row, -1.0
        )
        pos_key[64 * a : 64 * a + 64, :] = jnp.where(
            found > 0.0, total(place) * 4.0 + token_of_row, -1.0
        )
    rollouts = roll_ref[...]
    widen = (iota((128, 512), 0) == iota((128, 512), 1) // 4).astype(F32).astype(BF16)
    high = dot((rollouts // 32).astype(F32).astype(BF16), widen)
    low = dot((rollouts % 32).astype(F32).astype(BF16), widen)
    col_key[...] = (high * 32.0 + low) * 4.0 + (iota((8, 512), 1) % 4).astype(F32)
    sums[...] = jnp.zeros_like(sums)
    loads[5].wait()

    def add_chunk(a):
        chosen = (row_key[...] == col_key[pl.ds(a, 1), :]).astype(F32).astype(BF16)
        part = cot_buf[pl.ds(pl.multiple_of(a * 512, 512), 512), :]
        sums[...] += dot(chosen, part)

    add_chunk(0)

    def first_axis(o, carry):
        zz = (z + RING + shift(o)) % RING
        yy = (y + RING + shift(o)) % RING
        arrive(0, zz, y)
        push(0, half_of(0, zz, y), zz, y, up_y)
        push(0, half_of(0, zz, y), zz, y, down_y)
        arrive(1, z, yy)
        push(1, half_of(1, z, yy), z, yy, up_z)
        push(1, half_of(1, z, yy), z, yy, down_z)
        add_chunk(o)
        return carry

    lax.fori_loop(1, RING, first_axis, 0)

    sum_out[...] = sums[...].astype(BF16)

    def routed(buf, peer):
        return buf.at[pl.ds(pl.multiple_of(peer * BLOCK, BLOCK), BLOCK), :]

    def exchange(out_buf, in_buf, send, recv):
        def step(i, carry):
            peer = (d + i) % GROUPS
            remote(
                routed(out_buf, peer), routed(in_buf, d), send, recv.at[d], {"dp": peer}
            ).start()
            return carry

        lax.fori_loop(1, GROUPS, step, 0)
        here = pl.ds(pl.multiple_of(d * BLOCK, BLOCK), BLOCK)
        in_buf[here, :] = out_buf[here, :]

    def exchanged(out_buf, in_buf, send, recv):
        def step(i, carry):
            peer = (d + i) % GROUPS
            remote(
                routed(out_buf, peer), routed(in_buf, peer), send, recv.at[peer], {"dp": peer}
            ).wait_recv()
            return carry

        lax.fori_loop(1, GROUPS, step, 0)

    exchange(sum_out, sum_in, sum_send, sum_recv)

    def hop(h, o, up, down):
        zz = (z + RING + shift(o)) % RING
        yy = (y + RING + shift(o)) % RING
        below, above = (y + RING - h) % RING, (y + h) % RING
        arrive(0, zz, below)
        if up:
            push(0, half_of(0, zz, below), zz, below, up_y)
        arrive(0, zz, above)
        if down:
            push(0, half_of(0, zz, above), zz, above, down_y)
        below, above = (z + RING - h) % RING, (z + h) % RING
        arrive(1, below, yy)
        if up:
            push(1, half_of(1, below, yy), below, yy, up_z)
        arrive(1, above, yy)
        if down:
            push(1, half_of(1, above, yy), above, yy, down_z)

    def near_hops(i, carry):
        hop(i // RING + 1, i % RING, True, True)
        return carry

    lax.fori_loop(0, 2 * RING, near_hops, 0)

    def third_hop(i, carry):
        hop(3, 2 * i, True, False)
        hop(3, 2 * i + 1, False, True)
        return carry

    lax.fori_loop(0, RING // 2, third_hop, 0)

    own_half = (d % 2) * MEMBERS
    own_dest = jnp.sum(
        jnp.where(sub8 == d // 2, groups.astype(F32), 0.0), axis=0, keepdims=True
    )
    lane = iota((TOKENS, 128), 1)
    own_lane = own_half + iota((TOKENS, 128), 0) // 4
    dest = jnp.sum(jnp.where(lane == own_lane, own_dest, 0.0), axis=1, keepdims=True)
    same = (own_dest == dest) & (lane >= own_half) & (lane < own_lane)
    rank = jnp.sum(jnp.where(same, 1.0, 0.0), axis=1, keepdims=True)
    token = (iota((TOKENS, 1), 0) % 4).astype(F32)
    slot_row = dest * BLOCK + rank * 4.0 + token
    pick[...] = (slot_row == iota((TOKENS, ROUTED), 1).astype(F32)).astype(F32).astype(BF16)
    for load in loads[6:]:
        load.wait()

    def last_hop(o, carry):
        arrive(0, (z + RING + shift(o)) % RING, (y + 4) % RING)
        arrive(1, (z + 4) % RING, (y + RING + shift(o)) % RING)
        return carry

    lax.fori_loop(0, RING, last_hop, 0)

    def project(b, carry):
        here = pl.ds(pl.multiple_of(b * 128, 128), 128)
        product = dot(rows[here, :], w_buf[...])
        for j in range(4):
            wide[j, here, :] = product[:, j * COLS : (j + 1) * COLS]
        return carry

    lax.fori_loop(0, ROWS // 128, project, 0)
    outputs = wide[0, pl.ds(0, TOKENS, stride=4), :]
    for j in range(1, 4):
        outputs += wide[j, pl.ds(j, TOKENS, stride=4), :]
    hidden = outputs.astype(BF16).astype(F32)
    hidden_buf[...] = hidden
    gain = gain_ref[...]
    exchanged(sum_out, sum_in, sum_send, sum_recv)
    summed = dot(pick[...], sum_in[...])
    sums[0:TOKENS, :] = summed
    squares = jnp.sum((hidden * hidden).T, axis=0, keepdims=True)
    inner = jnp.sum((summed * gain * hidden).T, axis=0, keepdims=True)
    packet[0] = jnp.concatenate(
        [
            squares[:, 0:128],
            squares[:, 128:256],
            inner[:, 0:128],
            inner[:, 128:256],
            jnp.zeros((4, 128), F32),
        ],
        axis=0,
    )

    def share(slot, axis, me, in_buf, recv):
        def step(i, carry):
            remote(
                packet.at[slot],
                in_buf.at[me],
                stat_send.at[slot],
                recv.at[me],
                {axis: (me + i) % RING},
            ).start()
            return carry

        lax.fori_loop(1, RING, step, 0)
        in_buf[me] = packet[slot]

    def shared(slot, axis, me, in_buf, recv):
        def step(i, carry):
            peer = (me + i) % RING
            remote(
                packet.at[slot], in_buf.at[peer], stat_send.at[slot], recv.at[peer], {axis: peer}
            ).wait_recv()
            return carry

        lax.fori_loop(1, RING, step, 0)
        return jnp.sum(in_buf[...], axis=0)

    def turn(b, carry):
        here = pl.ds(pl.multiple_of(b * 128, 128), 128)
        rows_t[:, here] = rows[here, :].T
        return carry

    share(0, "mp", z, z_in, z_recv)
    lax.fori_loop(0, 4, turn, 0)
    packet[1] = shared(0, "mp", z, z_in, z_recv)
    share(1, "rep", y, y_in, y_recv)
    lax.fori_loop(4, 8, turn, 0)
    wide[...] = jnp.zeros_like(wide)
    totals = shared(1, "rep", y, y_in, y_recv)

    inverse_row = lax.rsqrt(totals[0:2, :] / D + EPSILON)
    scale_row = inverse_row * inverse_row * inverse_row / D * totals[2:4, :]
    turned = jnp.concatenate([inverse_row, scale_row, jnp.zeros((124, 128), F32)], axis=0).T
    inverse = jnp.concatenate([turned[:, 0:1], turned[:, 1:2]], axis=0)
    scale = jnp.concatenate([turned[:, 2:3], turned[:, 3:4]], axis=0)
    hidden = hidden_buf[...]
    token_grad = (inverse * gain * sums[0:TOKENS, :] - hidden * scale).astype(BF16).astype(F32)
    for j in range(4):
        wide[j, pl.ds(j, TOKENS, stride=4), :] = token_grad
    normed = (hidden * inverse * gain).astype(BF16)

    def narrow(b, carry):
        here = pl.ds(pl.multiple_of(b * 128, 128), 128)
        for j in range(4):
            spread[here, j * COLS : (j + 1) * COLS] = wide[j, here, :].astype(BF16)
        return carry

    lax.fori_loop(0, ROWS // 128, narrow, 0)

    partner = {"dp": 2 * x + 1 - core}

    def for_partner(i, carry):
        first = pl.multiple_of((1 - core + 2 * i) * PIECE, 64)
        here = pl.ds(pl.multiple_of(i * PIECE, 64), PIECE)
        pair_out[here, :] = dot(rows_t[pl.ds(first, PIECE), :], spread[...]).astype(BF16)
        remote(
            pair_out.at[here, :],
            pair_in.at[here, :],
            pair_send.at[i],
            pair_recv.at[i],
            partner,
        ).start()
        return carry

    lax.fori_loop(0, 2, for_partner, 0)

    def for_self(i, carry):
        first = pl.multiple_of((core + 2 * i) * PIECE, 64)
        here = pl.ds(pl.multiple_of(i * PIECE, 64), PIECE)
        kept[here, :] = dot(rows_t[pl.ds(first, PIECE), :], spread[...])
        return carry

    lax.fori_loop(0, 2, for_self, 0)

    def pair_arrived(i, carry):
        here = pl.ds(pl.multiple_of(i * PIECE, 64), PIECE)
        remote(
            pair_out.at[here, :], pair_in.at[here, :], pair_send.at[i], pair_recv.at[i], partner
        ).wait_recv()
        kept[here, :] = kept[here, :] + pair_in[here, :].astype(F32)
        return carry

    lax.fori_loop(0, 2, pair_arrived, 0)

    part = PIECE // 2
    ways = ((0, 1), (1, -1))

    def reach(way, half):
        return 4 if way == half else 3

    def kept_block(chip, half):
        first = pl.multiple_of((chip % 2) * PIECE + half * part, 32)
        return kept[pl.ds(first, part), pl.ds(pl.multiple_of((chip // 2) * COLS, COLS), COLS)]

    def chain(way, sign, half, step):
        return remote(
            chain_out.at[way, half, step],
            chain_in.at[way, half, step],
            chain_send.at[way, half, step],
            chain_recv.at[way, half, step],
            {"dp": 2 * ((x + RING + sign) % RING) + core},
        )

    for step in range(4):
        for half in range(2):
            for way, sign in ways:
                far = reach(way, half)
                if step >= far:
                    continue
                value = kept_block((x + RING + sign * (far - step)) % RING, half)
                if step:
                    chain(way, sign, half, step - 1).wait_recv()
                    value = value + chain_in[way, half, step - 1].astype(F32)
                chain_out[way, half, step] = value.astype(BF16)
                chain(way, sign, half, step).start()
        if step == 0:
            norm_out[...] = dot_first(pick[...], normed).astype(BF16)
            exchange(norm_out, norm_in, norm_send, norm_recv)

    exchanged(norm_out, norm_in, norm_send, norm_recv)
    home = (pos_key[...] == iota((ROUTED, TOKENS), 1).astype(F32)).astype(F32).astype(BF16)
    normed_out[...] = dot_first(home, norm_in[...]).astype(BF16)

    for half in range(2):
        value = kept_block(x, half)
        for way, sign in ways:
            last = reach(way, half) - 1
            chain(way, sign, half, last).wait_recv()
            value = value + chain_in[way, half, last].astype(F32)
        grad_out[half * part : (half + 1) * part, :] = value

    for half in range(2):
        sent = rows.at[pl.ds(0, (MEMBERS - 1) * SLOTS), pl.ds(half * HALF, HALF)]
        remote(
            sent, sent, gather_send.at[half], gather_recv.at[half, 0], {"rep": (y + 1) % RING}
        ).wait_send()
    sent = pl.ds(0, (GROUPS - 1) * BLOCK)
    for out_buf, send, recv in ((sum_out, sum_send, sum_recv), (norm_out, norm_send, norm_recv)):
        remote(
            out_buf.at[sent, :], out_buf.at[sent, :], send, recv.at[0], {"dp": (d + 1) % GROUPS}
        ).wait_send()
    sent = pl.ds(0, RING - 1)
    for slot, in_buf, recv in ((0, z_in, z_recv), (1, y_in, y_recv)):
        remote(
            in_buf.at[sent], in_buf.at[sent], stat_send.at[slot], recv.at[0], {"mp": (z + 1) % RING}
        ).wait_send()
    for i in range(2):
        here = pl.ds(i * PIECE, PIECE)
        remote(
            pair_out.at[here, :], pair_in.at[here, :], pair_send.at[i], pair_recv.at[i], partner
        ).wait_send()
    for half in range(2):
        for way, sign in ways:
            for step in range(reach(way, half)):
                chain(way, sign, half, step).wait_send()


def on_device(
    query_rows,
    key_rows,
    value_rows,
    residual,
    out_proj,
    merge_gain,
    merger_proj,
    model_gain,
    image_grid,
    image_group,
    rollout_image,
    cotangent,
):
    hbm = pl.BlockSpec(memory_space=pl.ANY)
    vmem = pl.BlockSpec(memory_space=pltpu.VMEM)
    dma = pltpu.SemaphoreType.DMA
    part = PIECE // 2
    return pl.pallas_call(
        kernel,
        out_shape=(
            jax.ShapeDtypeStruct((TOKENS, COLS), BF16),
            jax.ShapeDtypeStruct((PIECE, COLS), F32),
        ),
        in_specs=[hbm, hbm, hbm, hbm, hbm, vmem, hbm, vmem, vmem, vmem, vmem, hbm],
        out_specs=(vmem, vmem),
        scratch_shapes=[
            pltpu.VMEM((SLOTS, DV), BF16),
            pltpu.VMEM((SLOTS, DV), BF16),
            pltpu.VMEM((SLOTS, DV), BF16),
            pltpu.VMEM((SLOTS, DV), BF16),
            pltpu.VMEM((DV, DV), BF16),
            pltpu.VMEM((DV, 4 * COLS), BF16),
            pltpu.VMEM((4096, COLS), BF16),
            pltpu.VMEM((SLOTS, DV), BF16),
            pltpu.VMEM((ROWS, DV), BF16),
            pltpu.VMEM((DV, ROWS), BF16),
            pltpu.VMEM((4, ROWS, COLS), F32),
            pltpu.VMEM((ROWS, 4 * COLS), BF16),
            pltpu.VMEM((ROUTED, 1), F32),
            pltpu.VMEM((ROUTED, 1), F32),
            pltpu.VMEM((8, 512), F32),
            pltpu.VMEM((ROUTED, COLS), F32),
            pltpu.VMEM((ROUTED, COLS), BF16),
            pltpu.VMEM((ROUTED, COLS), BF16),
            pltpu.VMEM((TOKENS, ROUTED), BF16),
            pltpu.VMEM((TOKENS, COLS), F32),
            pltpu.VMEM((2, 8, 128), F32),
            pltpu.VMEM((RING, 8, 128), F32),
            pltpu.VMEM((RING, 8, 128), F32),
            pltpu.VMEM((ROUTED, COLS), BF16),
            pltpu.VMEM((ROUTED, COLS), BF16),
            pltpu.VMEM((2 * PIECE, 4 * COLS), F32),
            pltpu.VMEM((2 * PIECE, 4 * COLS), BF16),
            pltpu.VMEM((2 * PIECE, 4 * COLS), BF16),
            pltpu.VMEM((2, 2, 4, part, COLS), BF16),
            pltpu.VMEM((2, 2, 4, part, COLS), BF16),
            dma((10,)),
            dma((2,)),
            dma((2, MEMBERS)),
            dma,
            dma((GROUPS,)),
            dma((2,)),
            dma((RING,)),
            dma((RING,)),
            dma,
            dma((GROUPS,)),
            dma((2,)),
            dma((2,)),
            dma((2, 2, 4)),
            dma((2, 2, 4)),
        ],
        compiler_params=pltpu.CompilerParams(collective_id=0, has_side_effects=True),
        name="merge_step",
    )(
        query_rows,
        key_rows,
        value_rows,
        residual,
        out_proj,
        merge_gain.reshape(1, DV),
        merger_proj,
        model_gain.reshape(1, COLS),
        image_grid.T,
        image_group.reshape(8, 128),
        rollout_image.reshape(8, 128),
        cotangent,
    )


def solution(mesh):
    return jax.shard_map(
        on_device,
        mesh=mesh,
        in_specs=(
            P(("dp", "mp", "rep"), None),
            P(("dp", "mp", "rep"), None),
            P(("dp", "mp", "rep"), None),
            P(("dp", "mp", "rep"), None),
            P(),
            P(),
            P(None, ("mp", "rep")),
            P(("mp", "rep")),
            P(),
            P(),
            P("dp"),
            P("dp", ("mp", "rep")),
        ),
        out_specs=(P("dp", ("mp", "rep")), P("dp", ("mp", "rep"))),
        check_vma=False,
    )
```

```python
import functools

import jax
import jax.numpy as jnp
from jax import lax
from jax.experimental import pallas as pl
from jax.experimental.pallas import tpu as pltpu
from jax.sharding import PartitionSpec as P

HEADS = 16
HEAD = 80
DV = 1280
D = 8192
EPSILON = 1e-06
RING = 8
GROUPS = 16
MEMBERS = 64
SLOTS = 16
ROWS = MEMBERS * SLOTS
TOKENS = MEMBERS * 4
HALF = DV // 2
COLS = 128
BLOCK = 32
ROUTED = GROUPS * BLOCK
PIECE = 320
MESH = pl.DeviceIdType.MESH
F32 = jnp.float32
BF16 = jnp.bfloat16


def iota(shape, dim):
    return lax.broadcasted_iota(jnp.int32, shape, dim)


def dot(a, b):
    return jnp.dot(a, b, preferred_element_type=F32)


def dot_first(a, b):
    return lax.dot_general(a, b, (((0,), (0,)), ((), ())), preferred_element_type=F32)


def remote(src, dst, send, recv, device):
    return pltpu.make_async_remote_copy(
        src_ref=src,
        dst_ref=dst,
        send_sem=send,
        recv_sem=recv,
        device_id=device,
        device_id_type=MESH,
    )


def kernel(
    q_hbm,
    k_hbm,
    v_hbm,
    res_hbm,
    wo_hbm,
    merge_gain_ref,
    w_hbm,
    gain_ref,
    grid_ref,
    group_ref,
    roll_ref,
    cot_hbm,
    normed_out,
    grad_out,
    q_buf,
    k_buf,
    v_buf,
    res_buf,
    wo_buf,
    w_buf,
    cot_buf,
    own_buf,
    rows,
    rows_t,
    wide,
    spread,
    row_key,
    pos_key,
    col_key,
    sums,
    sum_out,
    sum_in,
    pick,
    hidden_buf,
    packet,
    z_in,
    y_in,
    norm_out,
    norm_in,
    kept,
    pair_out,
    pair_in,
    chain_out,
    chain_in,
    load_sem,
    gather_send,
    gather_recv,
    sum_send,
    sum_recv,
    stat_send,
    z_recv,
    y_recv,
    norm_send,
    norm_recv,
    pair_send,
    pair_recv,
    chain_send,
    chain_recv,
):
    d = lax.axis_index("dp")
    z = lax.axis_index("mp")
    y = lax.axis_index("rep")
    x = d // 2
    core = d % 2

    loads = [
        pltpu.make_async_copy(q_hbm, q_buf, load_sem.at[0]),
        pltpu.make_async_copy(k_hbm, k_buf, load_sem.at[1]),
        pltpu.make_async_copy(v_hbm, v_buf, load_sem.at[2]),
        pltpu.make_async_copy(res_hbm, res_buf, load_sem.at[3]),
        pltpu.make_async_copy(wo_hbm, wo_buf, load_sem.at[4]),
        pltpu.make_async_copy(cot_hbm, cot_buf, load_sem.at[5]),
    ] + [
        pltpu.make_async_copy(
            w_hbm.at[pl.ds(j * DV, DV), :], w_buf.at[:, pl.ds(j * COLS, COLS)], load_sem.at[6 + j]
        )
        for j in range(4)
    ]
    for load in loads:
        load.start()

    barrier = pltpu.get_barrier_semaphore()

    def greet(axis, me, size):
        def step(i, carry):
            pl.semaphore_signal(
                barrier, inc=1, device_id={axis: (me + i) % size}, device_id_type=MESH
            )
            return carry

        lax.fori_loop(1, size, step, 0)

    greet("mp", z, RING)
    greet("rep", y, RING)
    greet("dp", d, GROUPS)

    factors = grid_ref[...]
    products = factors[0:1, :] * factors[1:2, :]
    counts = jnp.concatenate(
        [products[:, 128 * a : 128 * a + 128] for a in range(8)], axis=0
    ).astype(F32)
    sub8 = iota((8, 128), 0)
    lane8 = iota((8, 128), 1)
    own_image = d * MEMBERS + z * RING + y
    is_own = (sub8 == own_image // 128) & (lane8 == own_image % 128)
    own_count = jnp.sum(
        jnp.sum(jnp.where(is_own, counts, 0.0), axis=0, keepdims=True), axis=1, keepdims=True
    )
    own_valid = own_count * 4.0

    loads[0].wait()
    loads[1].wait()
    head_of_row = iota((256, DV), 0) // SLOTS
    feature = iota((256, DV), 1)
    in_head = (feature >= head_of_row * HEAD) & (feature < head_of_row * HEAD + HEAD)
    queries = jnp.concatenate([q_buf[...].astype(F32)] * HEADS, axis=0)
    queries = jnp.where(in_head, queries, 0.0).astype(BF16)
    scores = lax.dot_general(
        queries, k_buf[...], (((1,), (1,)), ((), ())), preferred_element_type=F32
    ) * HEAD ** (-0.5)
    key_slot = iota((256, SLOTS), 1).astype(F32)
    scores = jnp.where(key_slot < own_valid, scores, -1e30)
    top = jnp.max(scores, axis=1, keepdims=True)
    powers = jnp.exp(scores - top)
    weights = (powers / jnp.sum(powers, axis=1, keepdims=True)).astype(BF16)
    loads[2].wait()
    attended = jnp.where(in_head, dot(weights, v_buf[...]), 0.0)
    attended = jnp.sum(attended.reshape(HEADS, SLOTS, DV), axis=0).astype(BF16)
    loads[3].wait()
    loads[4].wait()
    mixed = res_buf[...].astype(F32) + dot(attended, wo_buf[...])
    inverse_rms = lax.rsqrt(jnp.sum(mixed * mixed, axis=1, keepdims=True) / DV + EPSILON)
    slot_valid = (iota((SLOTS, 1), 0).astype(F32) < own_valid).astype(F32)
    merge_gain = jnp.concatenate([merge_gain_ref[i : i + 1, :] for i in range(10)], axis=1)
    own_buf[...] = (mixed * inverse_rms * merge_gain * slot_valid).astype(BF16)

    def image_rows(zz, yy):
        return pl.ds(pl.multiple_of((zz * RING + yy) * SLOTS, SLOTS), SLOTS)

    def half_of(half, zz, yy):
        return rows.at[image_rows(zz, yy), pl.ds(half * HALF, HALF)]

    pl.semaphore_wait(barrier, 2 * (RING - 1) + GROUPS - 1)

    def push(half, src, zz, yy, device):
        remote(
            src,
            half_of(half, zz, yy),
            gather_send.at[half],
            gather_recv.at[half, zz * RING + yy],
            device,
        ).start()

    def arrive(half, zz, yy):
        ref = half_of(half, zz, yy)
        remote(
            ref,
            ref,
            gather_send.at[half],
            gather_recv.at[half, zz * RING + yy],
            {"rep": (y + 1) % RING},
        ).wait_recv()

    up_y, down_y = {"rep": (y + 1) % RING}, {"rep": (y + RING - 1) % RING}
    up_z, down_z = {"mp": (z + 1) % RING}, {"mp": (z + RING - 1) % RING}
    own0 = own_buf.at[:, pl.ds(0, HALF)]
    own1 = own_buf.at[:, pl.ds(HALF, HALF)]

    def shift(o):
        return (1 - 2 * (o % 2)) * ((o + 1) // 2)

    push(0, own0, z, y, up_y)
    push(0, own0, z, y, down_y)
    push(1, own1, z, y, up_z)
    push(1, own1, z, y, down_z)

    def spread_own(o, carry):
        push(0, own0, z, y, {"mp": (z + RING + shift(o)) % RING})
        push(1, own1, z, y, {"rep": (y + RING + shift(o)) % RING})
        return carry

    lax.fori_loop(1, RING, spread_own, 0)
    rows[image_rows(z, y), :] = own_buf[...]

    groups = group_ref[...]
    arriving = groups == d
    arrived = arriving.astype(F32).astype(BF16)
    before = iota((128, 128), 0)
    after = iota((128, 128), 1)
    earlier = before < after
    rank_in_owner = dot(
        arrived, (earlier & (before // MEMBERS == after // MEMBERS)).astype(F32).astype(BF16)
    )
    rank_in_chunk = dot(arrived, earlier.astype(F32).astype(BF16))
    lower = (iota((8, 8), 0) > iota((8, 8), 1)).astype(F32).astype(BF16)
    chunk_start = jnp.sum(dot(lower, arrived), axis=1, keepdims=True)
    place = rank_in_chunk + chunk_start
    slot_in_chunk = jnp.where(
        arriving, (lane8 // MEMBERS).astype(F32) * 8.0 + rank_in_owner, -1.0
    )
    image_key = (sub8 * 128 + lane8).astype(F32) * 4.0
    slot_of_row = (iota((64, 128), 0) // 4).astype(F32)
    token_of_row = (iota((64, 1), 0) % 4).astype(F32)
    for a in range(8):
        match = slot_in_chunk[a : a + 1, :] == slot_of_row

        def total(value):
            return jnp.sum(jnp.where(match, value[a : a + 1, :], 0.0), axis=1, keepdims=True)

        found = total(counts)
        row_key[64 * a : 64 * a + 64, :] = jnp.where(
            token_of_row < found, total(image_key) + token_of_row, -1.0
        )
        pos_key[64 * a : 64 * a + 64, :] = jnp.where(
            found > 0.0, total(place) * 4.0 + token_of_row, -1.0
        )
    rollouts = roll_ref[...]
    widen = (iota((128, 512), 0) == iota((128, 512), 1) // 4).astype(F32).astype(BF16)
    high = dot((rollouts // 32).astype(F32).astype(BF16), widen)
    low = dot((rollouts % 32).astype(F32).astype(BF16), widen)
    col_key[...] = (high * 32.0 + low) * 4.0 + (iota((8, 512), 1) % 4).astype(F32)
    sums[...] = jnp.zeros_like(sums)
    loads[5].wait()

    def add_chunk(a):
        chosen = (row_key[...] == col_key[pl.ds(a, 1), :]).astype(F32).astype(BF16)
        part = cot_buf[pl.ds(pl.multiple_of(a * 512, 512), 512), :]
        sums[...] += dot(chosen, part)

    add_chunk(0)

    def first_axis(o):
        zz = (z + RING + shift(o)) % RING
        yy = (y + RING + shift(o)) % RING
        arrive(0, zz, y)
        push(0, half_of(0, zz, y), zz, y, up_y)
        push(0, half_of(0, zz, y), zz, y, down_y)
        arrive(1, z, yy)
        push(1, half_of(1, z, yy), z, yy, up_z)
        push(1, half_of(1, z, yy), z, yy, down_z)

    def first_axis_pair(i, carry):
        first_axis(2 * i + 1)
        first_axis(2 * i + 2)
        add_chunk(i + 1)
        return carry

    lax.fori_loop(0, 3, first_axis_pair, 0)
    first_axis(7)

    def hop(h, o, up, down):
        zz = (z + RING + shift(o)) % RING
        yy = (y + RING + shift(o)) % RING
        below, above = (y + RING - h) % RING, (y + h) % RING
        arrive(0, zz, below)
        if up:
            push(0, half_of(0, zz, below), zz, below, up_y)
        arrive(0, zz, above)
        if down:
            push(0, half_of(0, zz, above), zz, above, down_y)
        below, above = (z + RING - h) % RING, (z + h) % RING
        arrive(1, below, yy)
        if up:
            push(1, half_of(1, below, yy), below, yy, up_z)
        arrive(1, above, yy)
        if down:
            push(1, half_of(1, above, yy), above, yy, down_z)

    def first_hop(i, carry):
        hop(1, 2 * i, True, True)
        hop(1, 2 * i + 1, True, True)
        add_chunk(i + 4)
        return carry

    lax.fori_loop(0, RING // 2, first_hop, 0)

    sum_out[...] = sums[...].astype(BF16)

    def routed(buf, peer):
        return buf.at[pl.ds(pl.multiple_of(peer * BLOCK, BLOCK), BLOCK), :]

    def exchange(out_buf, in_buf, send, recv):
        def step(i, carry):
            peer = (d + i) % GROUPS
            remote(
                routed(out_buf, peer), routed(in_buf, d), send, recv.at[d], {"dp": peer}
            ).start()
            return carry

        lax.fori_loop(1, GROUPS, step, 0)
        here = pl.ds(pl.multiple_of(d * BLOCK, BLOCK), BLOCK)
        in_buf[here, :] = out_buf[here, :]

    def exchanged(out_buf, in_buf, send, recv):
        def step(i, carry):
            peer = (d + i) % GROUPS
            remote(
                routed(out_buf, peer), routed(in_buf, peer), send, recv.at[peer], {"dp": peer}
            ).wait_recv()
            return carry

        lax.fori_loop(1, GROUPS, step, 0)

    exchange(sum_out, sum_in, sum_send, sum_recv)

    def second_hop(o, carry):
        hop(2, o, True, True)
        return carry

    lax.fori_loop(0, RING, second_hop, 0)

    def third_hop(i, carry):
        hop(3, 2 * i, True, False)
        hop(3, 2 * i + 1, False, True)
        return carry

    lax.fori_loop(0, RING // 2, third_hop, 0)

    own_half = (d % 2) * MEMBERS
    own_dest = jnp.sum(
        jnp.where(sub8 == d // 2, groups.astype(F32), 0.0), axis=0, keepdims=True
    )
    lane = iota((TOKENS, 128), 1)
    own_lane = own_half + iota((TOKENS, 128), 0) // 4
    dest = jnp.sum(jnp.where(lane == own_lane, own_dest, 0.0), axis=1, keepdims=True)
    same = (own_dest == dest) & (lane >= own_half) & (lane < own_lane)
    rank = jnp.sum(jnp.where(same, 1.0, 0.0), axis=1, keepdims=True)
    token = (iota((TOKENS, 1), 0) % 4).astype(F32)
    slot_row = dest * BLOCK + rank * 4.0 + token
    pick[...] = (slot_row == iota((TOKENS, ROUTED), 1).astype(F32)).astype(F32).astype(BF16)
    for load in loads[6:]:
        load.wait()

    def last_hop(o, carry):
        zz = (z + RING + shift(o)) % RING
        arrive(0, zz, (y + 4) % RING)
        arrive(1, (z + 4) % RING, (y + RING + shift(o)) % RING)
        here = pl.ds(pl.multiple_of(zz * 128, 128), 128)
        product = dot(rows[here, :], w_buf[...])
        for j in range(4):
            wide[j, here, :] = product[:, j * COLS : (j + 1) * COLS]
        return carry

    lax.fori_loop(0, RING, last_hop, 0)
    outputs = wide[0, pl.ds(0, TOKENS, stride=4), :]
    for j in range(1, 4):
        outputs += wide[j, pl.ds(j, TOKENS, stride=4), :]
    hidden = outputs.astype(BF16).astype(F32)
    hidden_buf[...] = hidden
    gain = gain_ref[...]
    exchanged(sum_out, sum_in, sum_send, sum_recv)
    summed = dot(pick[...], sum_in[...])
    sums[0:TOKENS, :] = summed
    squares = jnp.sum((hidden * hidden).T, axis=0, keepdims=True)
    inner = jnp.sum((summed * gain * hidden).T, axis=0, keepdims=True)
    packet[0] = jnp.concatenate(
        [
            squares[:, 0:128],
            squares[:, 128:256],
            inner[:, 0:128],
            inner[:, 128:256],
        ],
        axis=0,
    )

    def share(slot, axis, me, in_buf, recv):
        def step(i, carry):
            remote(
                packet.at[slot],
                in_buf.at[me],
                stat_send.at[slot],
                recv.at[me],
                {axis: (me + i) % RING},
            ).start()
            return carry

        lax.fori_loop(1, RING, step, 0)
        in_buf[me] = packet[slot]

    def shared(slot, axis, me, in_buf, recv):
        def step(i, carry):
            peer = (me + i) % RING
            remote(
                packet.at[slot], in_buf.at[peer], stat_send.at[slot], recv.at[peer], {axis: peer}
            ).wait_recv()
            return carry

        lax.fori_loop(1, RING, step, 0)
        return jnp.sum(in_buf[...], axis=0)

    def turn(b, carry):
        here = pl.ds(pl.multiple_of(b * 128, 128), 128)
        rows_t[:, here] = rows[here, :].T
        return carry

    share(0, "mp", z, z_in, z_recv)
    lax.fori_loop(0, 4, turn, 0)
    packet[1] = shared(0, "mp", z, z_in, z_recv)
    share(1, "rep", y, y_in, y_recv)
    lax.fori_loop(4, 8, turn, 0)
    wide[...] = jnp.zeros_like(wide)
    totals = shared(1, "rep", y, y_in, y_recv)

    inverse_row = lax.rsqrt(totals[0:2, :] / D + EPSILON)
    scale_row = inverse_row * inverse_row * inverse_row / D * totals[2:4, :]
    turned = jnp.concatenate([inverse_row, scale_row, jnp.zeros((124, 128), F32)], axis=0).T
    inverse = jnp.concatenate([turned[:, 0:1], turned[:, 1:2]], axis=0)
    scale = jnp.concatenate([turned[:, 2:3], turned[:, 3:4]], axis=0)
    hidden = hidden_buf[...]
    token_grad = (inverse * gain * sums[0:TOKENS, :] - hidden * scale).astype(BF16).astype(F32)
    for j in range(4):
        wide[j, pl.ds(j, TOKENS, stride=4), :] = token_grad
    normed = (hidden * inverse * gain).astype(BF16)

    def narrow(b, carry):
        here = pl.ds(pl.multiple_of(b * 128, 128), 128)
        for j in range(4):
            spread[here, j * COLS : (j + 1) * COLS] = wide[j, here, :].astype(BF16)
        return carry

    lax.fori_loop(0, ROWS // 128, narrow, 0)

    partner = {"dp": 2 * x + 1 - core}
    offsets = ((4, 0), (3, 5), (2, 6), (1, 7))
    part = PIECE // 2
    ways = ((0, 1), (1, -1))

    def group_dot(group, owner):
        near, far = ((x + offset) % RING for offset in offsets[group])
        first = pl.multiple_of((near % 2) * (2 * PIECE) + owner * PIECE, 64)
        left = spread[:, pl.ds(pl.multiple_of((near // 2) * COLS, COLS), COLS)]
        right = spread[:, pl.ds(pl.multiple_of((far // 2) * COLS, COLS), COLS)]
        return dot(rows_t[pl.ds(first, PIECE), :], jnp.concatenate([left, right], axis=1))

    def pair(group):
        return remote(
            pair_out.at[group], pair_in.at[group], pair_send.at[group], pair_recv.at[group], partner
        )

    def reach(way, half):
        return 4 if way == half else 3

    def chain(way, sign, half, step):
        return remote(
            chain_out.at[way, half, step],
            chain_in.at[way, half, step],
            chain_send.at[way, half, step],
            chain_recv.at[way, half, step],
            {"dp": 2 * ((x + RING + sign) % RING) + core},
        )

    places = {offset: (g, i) for g, two in enumerate(offsets) for i, offset in enumerate(two)}

    def kept_block(offset, half):
        group, side = places[offset % RING]
        return kept[group, half * part : (half + 1) * part, side * COLS : (side + 1) * COLS]

    def link(way, sign, half, step):
        far = reach(way, half)
        value = kept_block(sign * (far - step), half)
        if step:
            chain(way, sign, half, step - 1).wait_recv()
            value = value + chain_in[way, half, step - 1].astype(F32)
        chain_out[way, half, step] = value.astype(BF16)
        chain(way, sign, half, step).start()

    def finish_group(group):
        pair(group).wait_recv()
        kept[group] = kept[group] + pair_in[group].astype(F32)

    for group in range(4):
        pair_out[group] = group_dot(group, 1 - core).astype(BF16)
        pair(group).start()
        kept[group] = group_dot(group, core)
    finish_group(0)
    for way, sign in ways:
        link(way, sign, way, 0)
    finish_group(1)
    for way, sign in ways:
        link(way, sign, 1 - way, 0)
    finish_group(2)
    finish_group(3)
    norm_out[...] = dot_first(pick[...], normed).astype(BF16)
    exchange(norm_out, norm_in, norm_send, norm_recv)
    for step in range(1, 4):
        for way, sign in ways:
            link(way, sign, way, step)
        if step < 3:
            for way, sign in ways:
                link(way, sign, 1 - way, step)
        if step == 2:
            exchanged(norm_out, norm_in, norm_send, norm_recv)
            home = pos_key[...] == iota((ROUTED, TOKENS), 1).astype(F32)
            home = home.astype(F32).astype(BF16)
            normed_out[...] = dot_first(home, norm_in[...]).astype(BF16)

    for half in range(2):
        value = kept_block(0, half)
        for way, sign in ways:
            last = reach(way, half) - 1
            chain(way, sign, half, last).wait_recv()
            value = value + chain_in[way, half, last].astype(F32)
        grad_out[half * part : (half + 1) * part, :] = value

    for half in range(2):
        sent = rows.at[pl.ds(0, (MEMBERS - 1) * SLOTS), pl.ds(half * HALF, HALF)]
        remote(
            sent, sent, gather_send.at[half], gather_recv.at[half, 0], {"rep": (y + 1) % RING}
        ).wait_send()
    sent = pl.ds(0, (GROUPS - 1) * BLOCK)
    for out_buf, send, recv in ((sum_out, sum_send, sum_recv), (norm_out, norm_send, norm_recv)):
        remote(
            out_buf.at[sent, :], out_buf.at[sent, :], send, recv.at[0], {"dp": (d + 1) % GROUPS}
        ).wait_send()
    sent = pl.ds(0, RING - 1)
    for slot, in_buf, recv in ((0, z_in, z_recv), (1, y_in, y_recv)):
        remote(
            in_buf.at[sent], in_buf.at[sent], stat_send.at[slot], recv.at[0], {"mp": (z + 1) % RING}
        ).wait_send()
    for group in range(4):
        pair(group).wait_send()
    for half in range(2):
        for way, sign in ways:
            for step in range(reach(way, half)):
                chain(way, sign, half, step).wait_send()


def on_device(
    query_rows,
    key_rows,
    value_rows,
    residual,
    out_proj,
    merge_gain,
    merger_proj,
    model_gain,
    image_grid,
    image_group,
    rollout_image,
    cotangent,
):
    hbm = pl.BlockSpec(memory_space=pl.ANY)
    vmem = pl.BlockSpec(memory_space=pltpu.VMEM)
    dma = pltpu.SemaphoreType.DMA
    part = PIECE // 2
    return pl.pallas_call(
        kernel,
        out_shape=(
            jax.ShapeDtypeStruct((TOKENS, COLS), BF16),
            jax.ShapeDtypeStruct((PIECE, COLS), F32),
        ),
        in_specs=[hbm, hbm, hbm, hbm, hbm, vmem, hbm, vmem, vmem, vmem, vmem, hbm],
        out_specs=(vmem, vmem),
        scratch_shapes=[
            pltpu.VMEM((SLOTS, DV), BF16),
            pltpu.VMEM((SLOTS, DV), BF16),
            pltpu.VMEM((SLOTS, DV), BF16),
            pltpu.VMEM((SLOTS, DV), BF16),
            pltpu.VMEM((DV, DV), BF16),
            pltpu.VMEM((DV, 4 * COLS), BF16),
            pltpu.VMEM((4096, COLS), BF16),
            pltpu.VMEM((SLOTS, DV), BF16),
            pltpu.VMEM((ROWS, DV), BF16),
            pltpu.VMEM((DV, ROWS), BF16),
            pltpu.VMEM((4, ROWS, COLS), F32),
            pltpu.VMEM((ROWS, 4 * COLS), BF16),
            pltpu.VMEM((ROUTED, 1), F32),
            pltpu.VMEM((ROUTED, 1), F32),
            pltpu.VMEM((8, 512), F32),
            pltpu.VMEM((ROUTED, COLS), F32),
            pltpu.VMEM((ROUTED, COLS), BF16),
            pltpu.VMEM((ROUTED, COLS), BF16),
            pltpu.VMEM((TOKENS, ROUTED), BF16),
            pltpu.VMEM((TOKENS, COLS), F32),
            pltpu.VMEM((2, 4, 128), F32),
            pltpu.VMEM((RING, 4, 128), F32),
            pltpu.VMEM((RING, 4, 128), F32),
            pltpu.VMEM((ROUTED, COLS), BF16),
            pltpu.VMEM((ROUTED, COLS), BF16),
            pltpu.VMEM((4, PIECE, 2 * COLS), F32),
            pltpu.VMEM((4, PIECE, 2 * COLS), BF16),
            pltpu.VMEM((4, PIECE, 2 * COLS), BF16),
            pltpu.VMEM((2, 2, 4, part, COLS), BF16),
            pltpu.VMEM((2, 2, 4, part, COLS), BF16),
            dma((10,)),
            dma((2,)),
            dma((2, MEMBERS)),
            dma,
            dma((GROUPS,)),
            dma((2,)),
            dma((RING,)),
            dma((RING,)),
            dma,
            dma((GROUPS,)),
            dma((4,)),
            dma((4,)),
            dma((2, 2, 4)),
            dma((2, 2, 4)),
        ],
        compiler_params=pltpu.CompilerParams(collective_id=0, has_side_effects=True),
        name="merge_step",
    )(
        query_rows,
        key_rows,
        value_rows,
        residual,
        out_proj,
        merge_gain.reshape(10, 128),
        merger_proj,
        model_gain.reshape(1, COLS),
        image_grid.T,
        image_group.reshape(8, 128),
        rollout_image.reshape(8, 128),
        cotangent,
    )


def solution(mesh):
    return jax.shard_map(
        on_device,
        mesh=mesh,
        in_specs=(
            P(("dp", "mp", "rep"), None),
            P(("dp", "mp", "rep"), None),
            P(("dp", "mp", "rep"), None),
            P(("dp", "mp", "rep"), None),
            P(),
            P(),
            P(None, ("mp", "rep")),
            P(("mp", "rep")),
            P(),
            P(),
            P("dp"),
            P("dp", ("mp", "rep")),
        ),
        out_specs=(P("dp", ("mp", "rep")), P("dp", ("mp", "rep"))),
        check_vma=False,
    )
```

```python
import functools

import jax
import jax.numpy as jnp
from jax import lax
from jax.experimental import pallas as pl
from jax.experimental.pallas import tpu as pltpu
from jax.sharding import PartitionSpec as P

HEADS = 16
HEAD = 80
DV = 1280
D = 8192
EPSILON = 1e-06
RING = 8
GROUPS = 16
MEMBERS = 64
SLOTS = 16
ROWS = MEMBERS * SLOTS
TOKENS = MEMBERS * 4
HALF = DV // 2
COLS = 128
BLOCK = 32
ROUTED = GROUPS * BLOCK
PIECE = 320
MESH = pl.DeviceIdType.MESH
F32 = jnp.float32
BF16 = jnp.bfloat16


def iota(shape, dim):
    return lax.broadcasted_iota(jnp.int32, shape, dim)


def dot(a, b):
    return jnp.dot(a, b, preferred_element_type=F32)


def dot_first(a, b):
    return lax.dot_general(a, b, (((0,), (0,)), ((), ())), preferred_element_type=F32)


def remote(src, dst, send, recv, device):
    return pltpu.make_async_remote_copy(
        src_ref=src,
        dst_ref=dst,
        send_sem=send,
        recv_sem=recv,
        device_id=device,
        device_id_type=MESH,
    )


def kernel(
    q_hbm,
    k_hbm,
    v_hbm,
    res_hbm,
    wo_hbm,
    merge_gain_ref,
    w_hbm,
    gain_ref,
    grid_ref,
    group_ref,
    roll_ref,
    cot_hbm,
    normed_out,
    grad_out,
    q_buf,
    k_buf,
    v_buf,
    res_buf,
    wo_buf,
    w_buf,
    cot_buf,
    own_buf,
    rows,
    rows_t,
    wide,
    spread,
    row_key,
    pos_key,
    col_key,
    sums,
    sum_out,
    sum_in,
    pick,
    hidden_buf,
    packet,
    z_in,
    y_in,
    norm_out,
    norm_in,
    kept,
    rows_p,
    grad_pair,
    chain_out,
    chain_in,
    load_sem,
    gather_send,
    gather_recv,
    sum_send,
    sum_recv,
    stat_send,
    z_recv,
    y_recv,
    norm_send,
    norm_recv,
    turn_send,
    turn_recv,
    pair_send,
    pair_recv,
    chain_send,
    chain_recv,
):
    d = lax.axis_index("dp")
    z = lax.axis_index("mp")
    y = lax.axis_index("rep")
    x = d // 2
    core = d % 2

    loads = [
        pltpu.make_async_copy(q_hbm, q_buf, load_sem.at[0]),
        pltpu.make_async_copy(k_hbm, k_buf, load_sem.at[1]),
        pltpu.make_async_copy(v_hbm, v_buf, load_sem.at[2]),
        pltpu.make_async_copy(res_hbm, res_buf, load_sem.at[3]),
        pltpu.make_async_copy(wo_hbm, wo_buf, load_sem.at[4]),
        pltpu.make_async_copy(cot_hbm, cot_buf, load_sem.at[5]),
    ] + [
        pltpu.make_async_copy(
            w_hbm.at[pl.ds(j * DV, DV), :], w_buf.at[:, pl.ds(j * COLS, COLS)], load_sem.at[6 + j]
        )
        for j in range(4)
    ]
    for load in loads:
        load.start()

    barrier = pltpu.get_barrier_semaphore()

    def greet(axis, me, size):
        def step(i, carry):
            pl.semaphore_signal(
                barrier, inc=1, device_id={axis: (me + i) % size}, device_id_type=MESH
            )
            return carry

        lax.fori_loop(1, size, step, 0)

    greet("mp", z, RING)
    greet("rep", y, RING)
    greet("dp", d, GROUPS)

    factors = grid_ref[...]
    products = factors[0:1, :] * factors[1:2, :]
    counts = jnp.concatenate(
        [products[:, 128 * a : 128 * a + 128] for a in range(8)], axis=0
    ).astype(F32)
    sub8 = iota((8, 128), 0)
    lane8 = iota((8, 128), 1)
    own_image = d * MEMBERS + z * RING + y
    is_own = (sub8 == own_image // 128) & (lane8 == own_image % 128)
    own_count = jnp.sum(
        jnp.sum(jnp.where(is_own, counts, 0.0), axis=0, keepdims=True), axis=1, keepdims=True
    )
    own_valid = own_count * 4.0

    loads[0].wait()
    loads[1].wait()
    head_of_row = iota((256, DV), 0) // SLOTS
    feature = iota((256, DV), 1)
    in_head = (feature >= head_of_row * HEAD) & (feature < head_of_row * HEAD + HEAD)
    queries = jnp.concatenate([q_buf[...].astype(F32)] * HEADS, axis=0)
    queries = jnp.where(in_head, queries, 0.0).astype(BF16)
    scores = lax.dot_general(
        queries, k_buf[...], (((1,), (1,)), ((), ())), preferred_element_type=F32
    ) * HEAD ** (-0.5)
    key_slot = iota((256, SLOTS), 1).astype(F32)
    scores = jnp.where(key_slot < own_valid, scores, -1e30)
    top = jnp.max(scores, axis=1, keepdims=True)
    powers = jnp.exp(scores - top)
    weights = (powers / jnp.sum(powers, axis=1, keepdims=True)).astype(BF16)
    loads[2].wait()
    attended = jnp.where(in_head, dot(weights, v_buf[...]), 0.0)
    attended = jnp.sum(attended.reshape(HEADS, SLOTS, DV), axis=0).astype(BF16)
    loads[3].wait()
    loads[4].wait()
    mixed = res_buf[...].astype(F32) + dot(attended, wo_buf[...])
    inverse_rms = lax.rsqrt(jnp.sum(mixed * mixed, axis=1, keepdims=True) / DV + EPSILON)
    slot_valid = (iota((SLOTS, 1), 0).astype(F32) < own_valid).astype(F32)
    merge_gain = jnp.concatenate([merge_gain_ref[i : i + 1, :] for i in range(10)], axis=1)
    own_buf[...] = (mixed * inverse_rms * merge_gain * slot_valid).astype(BF16)

    def image_rows(zz, yy):
        return pl.ds(pl.multiple_of((zz * RING + yy) * SLOTS, SLOTS), SLOTS)

    def half_of(half, zz, yy):
        return rows.at[image_rows(zz, yy), pl.ds(half * HALF, HALF)]

    pl.semaphore_wait(barrier, 2 * (RING - 1) + GROUPS - 1)

    def push(half, src, zz, yy, device):
        remote(
            src,
            half_of(half, zz, yy),
            gather_send.at[half],
            gather_recv.at[half, zz * RING + yy],
            device,
        ).start()

    def arrive(half, zz, yy):
        ref = half_of(half, zz, yy)
        remote(
            ref,
            ref,
            gather_send.at[half],
            gather_recv.at[half, zz * RING + yy],
            {"rep": (y + 1) % RING},
        ).wait_recv()

    up_y, down_y = {"rep": (y + 1) % RING}, {"rep": (y + RING - 1) % RING}
    up_z, down_z = {"mp": (z + 1) % RING}, {"mp": (z + RING - 1) % RING}
    own0 = own_buf.at[:, pl.ds(0, HALF)]
    own1 = own_buf.at[:, pl.ds(HALF, HALF)]

    def shift(o):
        return (1 - 2 * (o % 2)) * ((o + 1) // 2)

    push(0, own0, z, y, up_y)
    push(0, own0, z, y, down_y)
    push(1, own1, z, y, up_z)
    push(1, own1, z, y, down_z)

    def spread_own(o, carry):
        push(0, own0, z, y, {"mp": (z + RING + shift(o)) % RING})
        push(1, own1, z, y, {"rep": (y + RING + shift(o)) % RING})
        return carry

    lax.fori_loop(1, RING, spread_own, 0)
    rows[image_rows(z, y), :] = own_buf[...]

    partner = {"dp": 2 * x + 1 - core}

    def finish_plane(plane):
        here = pl.ds(pl.multiple_of(plane * 128, 128), 128)
        product = dot(rows[here, :], w_buf[...])
        for j in range(4):
            wide[j, here, :] = product[:, j * COLS : (j + 1) * COLS]
        rows_t[:, here] = rows[here, :].T
        for t in range(2):
            first = pl.multiple_of(2 * PIECE * t + (1 - core) * PIECE, 64)
            remote(
                rows_t.at[pl.ds(first, PIECE), here],
                rows_p.at[pl.ds(t * PIECE, PIECE), here],
                turn_send,
                turn_recv,
                partner,
            ).start()

    groups = group_ref[...]
    arriving = groups == d
    arrived = arriving.astype(F32).astype(BF16)
    before = iota((128, 128), 0)
    after = iota((128, 128), 1)
    earlier = before < after
    rank_in_owner = dot(
        arrived, (earlier & (before // MEMBERS == after // MEMBERS)).astype(F32).astype(BF16)
    )
    rank_in_chunk = dot(arrived, earlier.astype(F32).astype(BF16))
    lower = (iota((8, 8), 0) > iota((8, 8), 1)).astype(F32).astype(BF16)
    chunk_start = jnp.sum(dot(lower, arrived), axis=1, keepdims=True)
    place = rank_in_chunk + chunk_start
    slot_in_chunk = jnp.where(
        arriving, (lane8 // MEMBERS).astype(F32) * 8.0 + rank_in_owner, -1.0
    )
    image_key = (sub8 * 128 + lane8).astype(F32) * 4.0
    slot_of_row = (iota((64, 128), 0) // 4).astype(F32)
    token_of_row = (iota((64, 1), 0) % 4).astype(F32)
    for a in range(8):
        match = slot_in_chunk[a : a + 1, :] == slot_of_row

        def total(value):
            return jnp.sum(jnp.where(match, value[a : a + 1, :], 0.0), axis=1, keepdims=True)

        found = total(counts)
        row_key[64 * a : 64 * a + 64, :] = jnp.where(
            token_of_row < found, total(image_key) + token_of_row, -1.0
        )
        pos_key[64 * a : 64 * a + 64, :] = jnp.where(
            found > 0.0, total(place) * 4.0 + token_of_row, -1.0
        )
    rollouts = roll_ref[...]
    widen = (iota((128, 512), 0) == iota((128, 512), 1) // 4).astype(F32).astype(BF16)
    high = dot((rollouts // 32).astype(F32).astype(BF16), widen)
    low = dot((rollouts % 32).astype(F32).astype(BF16), widen)
    col_key[...] = (high * 32.0 + low) * 4.0 + (iota((8, 512), 1) % 4).astype(F32)
    sums[...] = jnp.zeros_like(sums)
    loads[5].wait()

    def add_chunk(a):
        chosen = (row_key[...] == col_key[pl.ds(a, 1), :]).astype(F32).astype(BF16)
        part = cot_buf[pl.ds(pl.multiple_of(a * 512, 512), 512), :]
        sums[...] += dot(chosen, part)

    add_chunk(0)

    def first_axis(o):
        zz = (z + RING + shift(o)) % RING
        yy = (y + RING + shift(o)) % RING
        arrive(0, zz, y)
        push(0, half_of(0, zz, y), zz, y, up_y)
        push(0, half_of(0, zz, y), zz, y, down_y)
        arrive(1, z, yy)
        push(1, half_of(1, z, yy), z, yy, up_z)
        push(1, half_of(1, z, yy), z, yy, down_z)

    def first_axis_pair(i, carry):
        first_axis(2 * i + 1)
        first_axis(2 * i + 2)
        add_chunk(i + 1)
        return carry

    lax.fori_loop(0, 3, first_axis_pair, 0)
    first_axis(7)

    def hop(h, o, up, down):
        zz = (z + RING + shift(o)) % RING
        yy = (y + RING + shift(o)) % RING
        below, above = (y + RING - h) % RING, (y + h) % RING
        arrive(0, zz, below)
        if up:
            push(0, half_of(0, zz, below), zz, below, up_y)
        arrive(0, zz, above)
        if down:
            push(0, half_of(0, zz, above), zz, above, down_y)
        below, above = (z + RING - h) % RING, (z + h) % RING
        arrive(1, below, yy)
        if up:
            push(1, half_of(1, below, yy), below, yy, up_z)
        arrive(1, above, yy)
        if down:
            push(1, half_of(1, above, yy), above, yy, down_z)

    def first_hop(i, carry):
        hop(1, 2 * i, True, True)
        hop(1, 2 * i + 1, True, True)
        add_chunk(i + 4)
        return carry

    lax.fori_loop(0, RING // 2, first_hop, 0)

    sum_out[...] = sums[...].astype(BF16)

    def routed(buf, peer):
        return buf.at[pl.ds(pl.multiple_of(peer * BLOCK, BLOCK), BLOCK), :]

    def exchange(out_buf, in_buf, send, recv):
        def step(i, carry):
            peer = (d + i) % GROUPS
            remote(
                routed(out_buf, peer), routed(in_buf, d), send, recv.at[d], {"dp": peer}
            ).start()
            return carry

        lax.fori_loop(1, GROUPS, step, 0)
        here = pl.ds(pl.multiple_of(d * BLOCK, BLOCK), BLOCK)
        in_buf[here, :] = out_buf[here, :]

    def exchanged(out_buf, in_buf, send, recv):
        def step(i, carry):
            peer = (d + i) % GROUPS
            remote(
                routed(out_buf, peer), routed(in_buf, peer), send, recv.at[peer], {"dp": peer}
            ).wait_recv()
            return carry

        lax.fori_loop(1, GROUPS, step, 0)

    exchange(sum_out, sum_in, sum_send, sum_recv)

    def second_hop(o, carry):
        hop(2, o, True, True)
        return carry

    lax.fori_loop(0, RING, second_hop, 0)

    def third_hop(i, carry):
        hop(3, 2 * i, True, False)
        hop(3, 2 * i + 1, False, True)
        return carry

    lax.fori_loop(0, RING // 2, third_hop, 0)

    own_half = (d % 2) * MEMBERS
    own_dest = jnp.sum(
        jnp.where(sub8 == d // 2, groups.astype(F32), 0.0), axis=0, keepdims=True
    )
    lane = iota((TOKENS, 128), 1)
    own_lane = own_half + iota((TOKENS, 128), 0) // 4
    dest = jnp.sum(jnp.where(lane == own_lane, own_dest, 0.0), axis=1, keepdims=True)
    same = (own_dest == dest) & (lane >= own_half) & (lane < own_lane)
    rank = jnp.sum(jnp.where(same, 1.0, 0.0), axis=1, keepdims=True)
    token = (iota((TOKENS, 1), 0) % 4).astype(F32)
    slot_row = dest * BLOCK + rank * 4.0 + token
    pick[...] = (slot_row == iota((TOKENS, ROUTED), 1).astype(F32)).astype(F32).astype(BF16)
    for load in loads[6:]:
        load.wait()

    def last_hop(o, carry):
        zz = (z + RING + shift(o)) % RING
        arrive(0, zz, (y + 4) % RING)
        arrive(1, (z + 4) % RING, (y + RING + shift(o)) % RING)
        finish_plane(zz)
        return carry

    lax.fori_loop(0, RING, last_hop, 0)
    outputs = wide[0, pl.ds(0, TOKENS, stride=4), :]
    for j in range(1, 4):
        outputs += wide[j, pl.ds(j, TOKENS, stride=4), :]
    hidden = outputs.astype(BF16).astype(F32)
    hidden_buf[...] = hidden
    gain = gain_ref[...]
    exchanged(sum_out, sum_in, sum_send, sum_recv)
    summed = dot(pick[...], sum_in[...])
    sums[0:TOKENS, :] = summed
    squares = jnp.sum((hidden * hidden).T, axis=0, keepdims=True)
    inner = jnp.sum((summed * gain * hidden).T, axis=0, keepdims=True)
    packet[0] = jnp.concatenate(
        [
            squares[:, 0:128],
            squares[:, 128:256],
            inner[:, 0:128],
            inner[:, 128:256],
        ],
        axis=0,
    )

    def share(slot, axis, me, in_buf, recv):
        def step(i, carry):
            remote(
                packet.at[slot],
                in_buf.at[me],
                stat_send.at[slot],
                recv.at[me],
                {axis: (me + i) % RING},
            ).start()
            return carry

        lax.fori_loop(1, RING, step, 0)
        in_buf[me] = packet[slot]

    def shared(slot, axis, me, in_buf, recv):
        def step(i, carry):
            peer = (me + i) % RING
            remote(
                packet.at[slot], in_buf.at[peer], stat_send.at[slot], recv.at[peer], {axis: peer}
            ).wait_recv()
            return carry

        lax.fori_loop(1, RING, step, 0)
        return jnp.sum(in_buf[...], axis=0)

    share(0, "mp", z, z_in, z_recv)
    wide[...] = jnp.zeros_like(wide)
    packet[1] = shared(0, "mp", z, z_in, z_recv)
    share(1, "rep", y, y_in, y_recv)
    totals = shared(1, "rep", y, y_in, y_recv)

    inverse_row = lax.rsqrt(totals[0:2, :] / D + EPSILON)
    scale_row = inverse_row * inverse_row * inverse_row / D * totals[2:4, :]
    turned = jnp.concatenate([inverse_row, scale_row, jnp.zeros((124, 128), F32)], axis=0).T
    inverse = jnp.concatenate([turned[:, 0:1], turned[:, 1:2]], axis=0)
    scale = jnp.concatenate([turned[:, 2:3], turned[:, 3:4]], axis=0)
    hidden = hidden_buf[...]
    token_grad = (inverse * gain * sums[0:TOKENS, :] - hidden * scale).astype(BF16)
    grad_pair[0] = token_grad
    grad_copy = remote(grad_pair.at[0], grad_pair.at[1], pair_send, pair_recv, partner)
    grad_copy.start()
    normed = (hidden * inverse * gain).astype(BF16)

    def spread_rows(grads, side):
        for j in range(4):
            wide[j, pl.ds(j, TOKENS, stride=4), :] = grads

        def narrow(b, carry):
            here = pl.ds(pl.multiple_of(b * 128, 128), 128)
            for j in range(4):
                spread[side, here, j * COLS : (j + 1) * COLS] = wide[j, here, :].astype(BF16)
            return carry

        lax.fori_loop(0, ROWS // 128, narrow, 0)

    offsets = ((4, 0), (3, 5), (2, 6), (1, 7))
    part = PIECE // 4
    ways = ((0, 1), (1, -1))

    def group_dot(group, side):
        near, far = ((x + offset) % RING for offset in offsets[group])
        left = spread[side, :, pl.ds(pl.multiple_of((near // 2) * COLS, COLS), COLS)]
        right = spread[side, :, pl.ds(pl.multiple_of((far // 2) * COLS, COLS), COLS)]
        both = jnp.concatenate([left, right], axis=1)
        if side == 0:
            first = pl.multiple_of((near % 2) * (2 * PIECE) + core * PIECE, 64)
            return dot(rows_t[pl.ds(first, PIECE), :], both)
        return dot(rows_p[pl.ds(pl.multiple_of((near % 2) * PIECE, 64), PIECE), :], both)

    def reach(way, half):
        return 4 if way == half else 3

    def chain(way, sign, half, chunk, step):
        return remote(
            chain_out.at[way, half, chunk, step],
            chain_in.at[way, half, chunk, step],
            chain_send.at[way, half, chunk, step],
            chain_recv.at[way, half, chunk, step],
            {"dp": 2 * ((x + RING + sign) % RING) + core},
        )

    places = {offset: (g, i) for g, two in enumerate(offsets) for i, offset in enumerate(two)}

    def kept_block(offset, half, chunk):
        group, side = places[offset % RING]
        first = (2 * half + chunk) * part
        return kept[group, first : first + part, side * COLS : (side + 1) * COLS]

    def link(long, step):
        for chunk in range(2):
            for way, sign in ways:
                half = way if long else 1 - way
                far = reach(way, half)
                value = kept_block(sign * (far - step), half, chunk)
                if step:
                    chain(way, sign, half, chunk, step - 1).wait_recv()
                    value = value + chain_in[way, half, chunk, step - 1].astype(F32)
                chain_out[way, half, chunk, step] = value.astype(BF16)
                chain(way, sign, half, chunk, step).start()

    spread_rows(token_grad.astype(F32), 0)
    for group in range(4):
        kept[group] = group_dot(group, 0)
    grad_copy.wait_recv()
    spread_rows(grad_pair[1].astype(F32), 1)
    remote(rows_p, rows_p, turn_send, turn_recv, partner).wait_recv()
    for group in range(4):
        kept[group] = kept[group] + group_dot(group, 1)
        if group == 0:
            link(True, 0)
        if group == 1:
            link(False, 0)
    norm_out[...] = dot_first(pick[...], normed).astype(BF16)
    exchange(norm_out, norm_in, norm_send, norm_recv)
    for step in range(1, 4):
        link(True, step)
        if step < 3:
            link(False, step)
        if step == 2:
            exchanged(norm_out, norm_in, norm_send, norm_recv)
            home = pos_key[...] == iota((ROUTED, TOKENS), 1).astype(F32)
            home = home.astype(F32).astype(BF16)
            normed_out[...] = dot_first(home, norm_in[...]).astype(BF16)

    for half in (1, 0):
        for chunk in range(2):
            value = kept_block(0, half, chunk)
            for way, sign in ways[:: -1 if half else 1]:
                last = reach(way, half) - 1
                chain(way, sign, half, chunk, last).wait_recv()
                value = value + chain_in[way, half, chunk, last].astype(F32)
            first = (2 * half + chunk) * part
            grad_out[first : first + part, :] = value

    for half in range(2):
        sent = rows.at[pl.ds(0, (MEMBERS - 1) * SLOTS), pl.ds(half * HALF, HALF)]
        remote(
            sent, sent, gather_send.at[half], gather_recv.at[half, 0], {"rep": (y + 1) % RING}
        ).wait_send()
    sent = pl.ds(0, (GROUPS - 1) * BLOCK)
    for out_buf, send, recv in ((sum_out, sum_send, sum_recv), (norm_out, norm_send, norm_recv)):
        remote(
            out_buf.at[sent, :], out_buf.at[sent, :], send, recv.at[0], {"dp": (d + 1) % GROUPS}
        ).wait_send()
    sent = pl.ds(0, RING - 1)
    for slot, in_buf, recv in ((0, z_in, z_recv), (1, y_in, y_recv)):
        remote(
            in_buf.at[sent], in_buf.at[sent], stat_send.at[slot], recv.at[0], {"mp": (z + 1) % RING}
        ).wait_send()
    grad_copy.wait_send()
    remote(rows_p, rows_p, turn_send, turn_recv, partner).wait_send()
    for half in range(2):
        for chunk in range(2):
            for way, sign in ways:
                for step in range(reach(way, half)):
                    chain(way, sign, half, chunk, step).wait_send()


def on_device(
    query_rows,
    key_rows,
    value_rows,
    residual,
    out_proj,
    merge_gain,
    merger_proj,
    model_gain,
    image_grid,
    image_group,
    rollout_image,
    cotangent,
):
    hbm = pl.BlockSpec(memory_space=pl.ANY)
    vmem = pl.BlockSpec(memory_space=pltpu.VMEM)
    dma = pltpu.SemaphoreType.DMA
    part = PIECE // 4
    return pl.pallas_call(
        kernel,
        out_shape=(
            jax.ShapeDtypeStruct((TOKENS, COLS), BF16),
            jax.ShapeDtypeStruct((PIECE, COLS), F32),
        ),
        in_specs=[hbm, hbm, hbm, hbm, hbm, vmem, hbm, vmem, vmem, vmem, vmem, hbm],
        out_specs=(vmem, vmem),
        scratch_shapes=[
            pltpu.VMEM((SLOTS, DV), BF16),
            pltpu.VMEM((SLOTS, DV), BF16),
            pltpu.VMEM((SLOTS, DV), BF16),
            pltpu.VMEM((SLOTS, DV), BF16),
            pltpu.VMEM((DV, DV), BF16),
            pltpu.VMEM((DV, 4 * COLS), BF16),
            pltpu.VMEM((4096, COLS), BF16),
            pltpu.VMEM((SLOTS, DV), BF16),
            pltpu.VMEM((ROWS, DV), BF16),
            pltpu.VMEM((DV, ROWS), BF16),
            pltpu.VMEM((4, ROWS, COLS), F32),
            pltpu.VMEM((2, ROWS, 4 * COLS), BF16),
            pltpu.VMEM((ROUTED, 1), F32),
            pltpu.VMEM((ROUTED, 1), F32),
            pltpu.VMEM((8, 512), F32),
            pltpu.VMEM((ROUTED, COLS), F32),
            pltpu.VMEM((ROUTED, COLS), BF16),
            pltpu.VMEM((ROUTED, COLS), BF16),
            pltpu.VMEM((TOKENS, ROUTED), BF16),
            pltpu.VMEM((TOKENS, COLS), F32),
            pltpu.VMEM((2, 4, 128), F32),
            pltpu.VMEM((RING, 4, 128), F32),
            pltpu.VMEM((RING, 4, 128), F32),
            pltpu.VMEM((ROUTED, COLS), BF16),
            pltpu.VMEM((ROUTED, COLS), BF16),
            pltpu.VMEM((4, PIECE, 2 * COLS), F32),
            pltpu.VMEM((2 * PIECE, ROWS), BF16),
            pltpu.VMEM((2, TOKENS, COLS), BF16),
            pltpu.VMEM((2, 2, 2, 4, part, COLS), BF16),
            pltpu.VMEM((2, 2, 2, 4, part, COLS), BF16),
            dma((10,)),
            dma((2,)),
            dma((2, MEMBERS)),
            dma,
            dma((GROUPS,)),
            dma((2,)),
            dma((RING,)),
            dma((RING,)),
            dma,
            dma((GROUPS,)),
            dma,
            dma,
            dma,
            dma,
            dma((2, 2, 2, 4)),
            dma((2, 2, 2, 4)),
        ],
        compiler_params=pltpu.CompilerParams(collective_id=0, has_side_effects=True),
        name="merge_step",
    )(
        query_rows,
        key_rows,
        value_rows,
        residual,
        out_proj,
        merge_gain.reshape(10, 128),
        merger_proj,
        model_gain.reshape(1, COLS),
        image_grid.T,
        image_group.reshape(8, 128),
        rollout_image.reshape(8, 128),
        cotangent,
    )


def solution(mesh):
    return jax.shard_map(
        on_device,
        mesh=mesh,
        in_specs=(
            P(("dp", "mp", "rep"), None),
            P(("dp", "mp", "rep"), None),
            P(("dp", "mp", "rep"), None),
            P(("dp", "mp", "rep"), None),
            P(),
            P(),
            P(None, ("mp", "rep")),
            P(("mp", "rep")),
            P(),
            P(),
            P("dp"),
            P("dp", ("mp", "rep")),
        ),
        out_specs=(P("dp", ("mp", "rep")), P("dp", ("mp", "rep"))),
        check_vma=False,
    )
```

```python
import functools

import jax
import jax.numpy as jnp
from jax import lax
from jax.experimental import pallas as pl
from jax.experimental.pallas import tpu as pltpu
from jax.sharding import PartitionSpec as P

HEADS = 16
HEAD = 80
DV = 1280
D = 8192
EPSILON = 1e-06
RING = 8
GROUPS = 16
MEMBERS = 64
SLOTS = 16
ROWS = MEMBERS * SLOTS
TOKENS = MEMBERS * 4
HALF = DV // 2
COLS = 128
BLOCK = 32
ROUTED = GROUPS * BLOCK
PIECE = 320
MESH = pl.DeviceIdType.MESH
F32 = jnp.float32
BF16 = jnp.bfloat16


def iota(shape, dim):
    return lax.broadcasted_iota(jnp.int32, shape, dim)


def dot(a, b):
    return jnp.dot(a, b, preferred_element_type=F32)


def dot_first(a, b):
    return lax.dot_general(a, b, (((0,), (0,)), ((), ())), preferred_element_type=F32)


def remote(src, dst, send, recv, device):
    return pltpu.make_async_remote_copy(
        src_ref=src,
        dst_ref=dst,
        send_sem=send,
        recv_sem=recv,
        device_id=device,
        device_id_type=MESH,
    )


def kernel(
    q_hbm,
    k_hbm,
    v_hbm,
    res_hbm,
    wo_hbm,
    merge_gain_hbm,
    w_hbm,
    gain_hbm,
    grid_hbm,
    group_hbm,
    roll_hbm,
    cot_hbm,
    normed_out,
    grad_out,
    merge_gain_ref,
    gain_ref,
    grid_ref,
    group_ref,
    roll_ref,
    q_buf,
    k_buf,
    v_buf,
    res_buf,
    wo_buf,
    w_buf,
    cot_buf,
    own_buf,
    rows,
    rows_t,
    wide,
    spread,
    row_key,
    pos_key,
    col_key,
    sums,
    sum_out,
    sum_in,
    pick,
    hidden_buf,
    packet,
    z_in,
    y_in,
    norm_out,
    norm_in,
    kept,
    rows_p,
    grad_pair,
    chain_out,
    chain_in,
    load_sem,
    gather_send,
    gather_recv,
    sum_send,
    sum_recv,
    stat_send,
    z_recv,
    y_recv,
    norm_send,
    norm_recv,
    turn_send,
    turn_recv,
    pair_send,
    pair_recv,
    chain_send,
    chain_recv,
):
    d = lax.axis_index("dp")
    z = lax.axis_index("mp")
    y = lax.axis_index("rep")
    x = d // 2
    core = d % 2

    smalls = [
        pltpu.make_async_copy(grid_hbm, grid_ref, load_sem.at[10]),
        pltpu.make_async_copy(merge_gain_hbm, merge_gain_ref, load_sem.at[11]),
        pltpu.make_async_copy(group_hbm, group_ref, load_sem.at[12]),
        pltpu.make_async_copy(roll_hbm, roll_ref, load_sem.at[13]),
        pltpu.make_async_copy(gain_hbm, gain_ref, load_sem.at[14]),
    ]
    loads = [
        pltpu.make_async_copy(q_hbm, q_buf, load_sem.at[0]),
        pltpu.make_async_copy(k_hbm, k_buf, load_sem.at[1]),
        pltpu.make_async_copy(v_hbm, v_buf, load_sem.at[2]),
        pltpu.make_async_copy(res_hbm, res_buf, load_sem.at[3]),
        pltpu.make_async_copy(wo_hbm, wo_buf, load_sem.at[4]),
        pltpu.make_async_copy(cot_hbm, cot_buf, load_sem.at[5]),
    ] + [
        pltpu.make_async_copy(
            w_hbm.at[pl.ds(j * DV, DV), :], w_buf.at[:, pl.ds(j * COLS, COLS)], load_sem.at[6 + j]
        )
        for j in range(4)
    ]
    smalls[0].start()
    for load in loads[:5] + smalls[1:] + loads[5:]:
        load.start()

    barrier = pltpu.get_barrier_semaphore()

    def greet(axis, me, size):
        def step(i, carry):
            pl.semaphore_signal(
                barrier, inc=1, device_id={axis: (me + i) % size}, device_id_type=MESH
            )
            return carry

        lax.fori_loop(1, size, step, 0)

    greet("mp", z, RING)
    greet("rep", y, RING)
    greet("dp", d, GROUPS)

    smalls[0].wait()
    factors = grid_ref[...]
    products = factors[0:1, :] * factors[1:2, :]
    counts = jnp.concatenate(
        [products[:, 128 * a : 128 * a + 128] for a in range(8)], axis=0
    ).astype(F32)
    sub8 = iota((8, 128), 0)
    lane8 = iota((8, 128), 1)
    own_image = d * MEMBERS + z * RING + y
    is_own = (sub8 == own_image // 128) & (lane8 == own_image % 128)
    own_count = jnp.sum(
        jnp.sum(jnp.where(is_own, counts, 0.0), axis=0, keepdims=True), axis=1, keepdims=True
    )
    own_valid = own_count * 4.0

    loads[0].wait()
    loads[1].wait()
    head_of_row = iota((256, DV), 0) // SLOTS
    feature = iota((256, DV), 1)
    in_head = (feature >= head_of_row * HEAD) & (feature < head_of_row * HEAD + HEAD)
    queries = jnp.concatenate([q_buf[...].astype(F32)] * HEADS, axis=0)
    queries = jnp.where(in_head, queries, 0.0).astype(BF16)
    scores = lax.dot_general(
        queries, k_buf[...], (((1,), (1,)), ((), ())), preferred_element_type=F32
    ) * HEAD ** (-0.5)
    key_slot = iota((256, SLOTS), 1).astype(F32)
    scores = jnp.where(key_slot < own_valid, scores, -1e30)
    top = jnp.max(scores, axis=1, keepdims=True)
    powers = jnp.exp(scores - top)
    weights = (powers / jnp.sum(powers, axis=1, keepdims=True)).astype(BF16)
    loads[2].wait()
    attended = jnp.where(in_head, dot(weights, v_buf[...]), 0.0)
    attended = jnp.sum(attended.reshape(HEADS, SLOTS, DV), axis=0).astype(BF16)
    loads[3].wait()
    loads[4].wait()
    mixed = res_buf[...].astype(F32) + dot(attended, wo_buf[...])
    inverse_rms = lax.rsqrt(jnp.sum(mixed * mixed, axis=1, keepdims=True) / DV + EPSILON)
    slot_valid = (iota((SLOTS, 1), 0).astype(F32) < own_valid).astype(F32)
    smalls[1].wait()
    merge_gain = jnp.concatenate([merge_gain_ref[i : i + 1, :] for i in range(10)], axis=1)
    own_buf[...] = (mixed * inverse_rms * merge_gain * slot_valid).astype(BF16)

    def image_rows(zz, yy):
        return pl.ds(pl.multiple_of((zz * RING + yy) * SLOTS, SLOTS), SLOTS)

    def half_of(half, zz, yy):
        return rows.at[image_rows(zz, yy), pl.ds(half * HALF, HALF)]

    pl.semaphore_wait(barrier, 2 * (RING - 1) + GROUPS - 1)

    def push(half, src, zz, yy, device):
        remote(
            src,
            half_of(half, zz, yy),
            gather_send.at[half],
            gather_recv.at[half, zz * RING + yy],
            device,
        ).start()

    def arrive(half, zz, yy):
        ref = half_of(half, zz, yy)
        remote(
            ref,
            ref,
            gather_send.at[half],
            gather_recv.at[half, zz * RING + yy],
            {"rep": (y + 1) % RING},
        ).wait_recv()

    up_y, down_y = {"rep": (y + 1) % RING}, {"rep": (y + RING - 1) % RING}
    up_z, down_z = {"mp": (z + 1) % RING}, {"mp": (z + RING - 1) % RING}
    own0 = own_buf.at[:, pl.ds(0, HALF)]
    own1 = own_buf.at[:, pl.ds(HALF, HALF)]

    def shift(o):
        return (1 - 2 * (o % 2)) * ((o + 1) // 2)

    push(0, own0, z, y, up_y)
    push(0, own0, z, y, down_y)
    push(1, own1, z, y, up_z)
    push(1, own1, z, y, down_z)

    def spread_own(o, carry):
        push(0, own0, z, y, {"mp": (z + RING + shift(o)) % RING})
        push(1, own1, z, y, {"rep": (y + RING + shift(o)) % RING})
        return carry

    lax.fori_loop(1, RING, spread_own, 0)
    rows[image_rows(z, y), :] = own_buf[...]

    partner = {"dp": 2 * x + 1 - core}

    def project(plane):
        here = pl.ds(pl.multiple_of(plane * 128, 128), 128)
        product = dot(rows[here, :], w_buf[...])
        for j in range(4):
            wide[j, here, :] = product[:, j * COLS : (j + 1) * COLS]

    def turn(half, plane):
        here = pl.ds(pl.multiple_of(plane * 128, 128), 128)
        features = slice(half * HALF, (half + 1) * HALF)
        rows_t[features, here] = rows[here, features].T
        first = pl.multiple_of(HALF * half + (1 - core) * PIECE, 64)
        remote(
            rows_t.at[pl.ds(first, PIECE), here],
            rows_p.at[pl.ds(half * PIECE, PIECE), here],
            turn_send,
            turn_recv,
            partner,
        ).start()

    for load in smalls[2:]:
        load.wait()
    groups = group_ref[...]
    arriving = groups == d
    arrived = arriving.astype(F32).astype(BF16)
    before = iota((128, 128), 0)
    after = iota((128, 128), 1)
    earlier = before < after
    rank_in_owner = dot(
        arrived, (earlier & (before // MEMBERS == after // MEMBERS)).astype(F32).astype(BF16)
    )
    rank_in_chunk = dot(arrived, earlier.astype(F32).astype(BF16))
    lower = (iota((8, 8), 0) > iota((8, 8), 1)).astype(F32).astype(BF16)
    chunk_start = jnp.sum(dot(lower, arrived), axis=1, keepdims=True)
    place = rank_in_chunk + chunk_start
    slot_in_chunk = jnp.where(
        arriving, (lane8 // MEMBERS).astype(F32) * 8.0 + rank_in_owner, -1.0
    )
    image_key = (sub8 * 128 + lane8).astype(F32) * 4.0
    slot_of_row = (iota((64, 128), 0) // 4).astype(F32)
    token_of_row = (iota((64, 1), 0) % 4).astype(F32)
    for a in range(8):
        match = slot_in_chunk[a : a + 1, :] == slot_of_row

        def total(value):
            return jnp.sum(jnp.where(match, value[a : a + 1, :], 0.0), axis=1, keepdims=True)

        found = total(counts)
        row_key[64 * a : 64 * a + 64, :] = jnp.where(
            token_of_row < found, total(image_key) + token_of_row, -1.0
        )
        pos_key[64 * a : 64 * a + 64, :] = jnp.where(
            found > 0.0, total(place) * 4.0 + token_of_row, -1.0
        )
    rollouts = roll_ref[...]
    widen = (iota((128, 512), 0) == iota((128, 512), 1) // 4).astype(F32).astype(BF16)
    high = dot((rollouts // 32).astype(F32).astype(BF16), widen)
    low = dot((rollouts % 32).astype(F32).astype(BF16), widen)
    col_key[...] = (high * 32.0 + low) * 4.0 + (iota((8, 512), 1) % 4).astype(F32)
    sums[...] = jnp.zeros_like(sums)
    loads[5].wait()

    def add_chunk(a):
        chosen = (row_key[...] == col_key[pl.ds(a, 1), :]).astype(F32).astype(BF16)
        part = cot_buf[pl.ds(pl.multiple_of(a * 512, 512), 512), :]
        sums[...] += dot(chosen, part)

    add_chunk(0)

    def first_axis(o):
        zz = (z + RING + shift(o)) % RING
        yy = (y + RING + shift(o)) % RING
        arrive(0, zz, y)
        push(0, half_of(0, zz, y), zz, y, up_y)
        push(0, half_of(0, zz, y), zz, y, down_y)
        arrive(1, z, yy)
        push(1, half_of(1, z, yy), z, yy, up_z)
        push(1, half_of(1, z, yy), z, yy, down_z)

    def first_axis_pair(i, carry):
        first_axis(2 * i + 1)
        first_axis(2 * i + 2)
        add_chunk(i + 1)
        return carry

    lax.fori_loop(0, 3, first_axis_pair, 0)
    first_axis(7)

    def hop(h, o, up, down):
        zz = (z + RING + shift(o)) % RING
        yy = (y + RING + shift(o)) % RING
        below, above = (y + RING - h) % RING, (y + h) % RING
        arrive(0, zz, below)
        if up:
            push(0, half_of(0, zz, below), zz, below, up_y)
        arrive(0, zz, above)
        if down:
            push(0, half_of(0, zz, above), zz, above, down_y)
        below, above = (z + RING - h) % RING, (z + h) % RING
        arrive(1, below, yy)
        if up:
            push(1, half_of(1, below, yy), below, yy, up_z)
        arrive(1, above, yy)
        if down:
            push(1, half_of(1, above, yy), above, yy, down_z)

    def first_hop(i, carry):
        hop(1, 2 * i, True, True)
        hop(1, 2 * i + 1, True, True)
        add_chunk(i + 4)
        return carry

    turn(1, z)
    lax.fori_loop(0, RING // 2, first_hop, 0)
    turn(1, (z + 1) % RING)
    turn(1, (z + 7) % RING)

    sum_out[...] = sums[...].astype(BF16)

    def routed(buf, peer):
        return buf.at[pl.ds(pl.multiple_of(peer * BLOCK, BLOCK), BLOCK), :]

    def exchange(out_buf, in_buf, send, recv):
        def step(i, carry):
            peer = (d + i) % GROUPS
            remote(
                routed(out_buf, peer), routed(in_buf, d), send, recv.at[d], {"dp": peer}
            ).start()
            return carry

        lax.fori_loop(1, GROUPS, step, 0)
        here = pl.ds(pl.multiple_of(d * BLOCK, BLOCK), BLOCK)
        in_buf[here, :] = out_buf[here, :]

    def exchanged(out_buf, in_buf, send, recv):
        def step(i, carry):
            peer = (d + i) % GROUPS
            remote(
                routed(out_buf, peer), routed(in_buf, peer), send, recv.at[peer], {"dp": peer}
            ).wait_recv()
            return carry

        lax.fori_loop(1, GROUPS, step, 0)

    exchange(sum_out, sum_in, sum_send, sum_recv)

    def second_hop(o, carry):
        hop(2, o, True, True)
        return carry

    lax.fori_loop(0, RING, second_hop, 0)
    turn(1, (z + 2) % RING)
    turn(1, (z + 6) % RING)

    def third_hop(i, carry):
        hop(3, 2 * i, True, False)
        hop(3, 2 * i + 1, False, True)
        return carry

    lax.fori_loop(0, RING // 2, third_hop, 0)
    turn(1, (z + 3) % RING)
    turn(1, (z + 5) % RING)

    own_half = (d % 2) * MEMBERS
    own_dest = jnp.sum(
        jnp.where(sub8 == d // 2, groups.astype(F32), 0.0), axis=0, keepdims=True
    )
    lane = iota((TOKENS, 128), 1)
    own_lane = own_half + iota((TOKENS, 128), 0) // 4
    dest = jnp.sum(jnp.where(lane == own_lane, own_dest, 0.0), axis=1, keepdims=True)
    same = (own_dest == dest) & (lane >= own_half) & (lane < own_lane)
    rank = jnp.sum(jnp.where(same, 1.0, 0.0), axis=1, keepdims=True)
    token = (iota((TOKENS, 1), 0) % 4).astype(F32)
    slot_row = dest * BLOCK + rank * 4.0 + token
    pick[...] = (slot_row == iota((TOKENS, ROUTED), 1).astype(F32)).astype(F32).astype(BF16)
    for load in loads[6:]:
        load.wait()

    def last_hop(o, carry):
        zz = (z + RING + shift(o)) % RING
        arrive(0, zz, (y + 4) % RING)
        arrive(1, (z + 4) % RING, (y + RING + shift(o)) % RING)
        turn(0, zz)
        project(zz)
        return carry

    lax.fori_loop(0, RING, last_hop, 0)
    turn(1, (z + 4) % RING)
    outputs = wide[0, pl.ds(0, TOKENS, stride=4), :]
    for j in range(1, 4):
        outputs += wide[j, pl.ds(j, TOKENS, stride=4), :]
    hidden = outputs.astype(BF16).astype(F32)
    hidden_buf[...] = hidden
    gain = gain_ref[...]
    exchanged(sum_out, sum_in, sum_send, sum_recv)
    summed = dot(pick[...], sum_in[...])
    sums[0:TOKENS, :] = summed
    squares = jnp.sum((hidden * hidden).T, axis=0, keepdims=True)
    inner = jnp.sum((summed * gain * hidden).T, axis=0, keepdims=True)
    packet[0] = jnp.concatenate(
        [
            squares[:, 0:128],
            squares[:, 128:256],
            inner[:, 0:128],
            inner[:, 128:256],
        ],
        axis=0,
    )

    def share(slot, axis, me, in_buf, recv):
        def step(i, carry):
            remote(
                packet.at[slot],
                in_buf.at[me],
                stat_send.at[slot],
                recv.at[me],
                {axis: (me + i) % RING},
            ).start()
            return carry

        lax.fori_loop(1, RING, step, 0)
        in_buf[me] = packet[slot]

    def shared(slot, axis, me, in_buf, recv):
        def step(i, carry):
            peer = (me + i) % RING
            remote(
                packet.at[slot], in_buf.at[peer], stat_send.at[slot], recv.at[peer], {axis: peer}
            ).wait_recv()
            return carry

        lax.fori_loop(1, RING, step, 0)
        return jnp.sum(in_buf[...], axis=0)

    share(0, "mp", z, z_in, z_recv)
    wide[...] = jnp.zeros_like(wide)
    packet[1] = shared(0, "mp", z, z_in, z_recv)
    share(1, "rep", y, y_in, y_recv)
    totals = shared(1, "rep", y, y_in, y_recv)

    inverse_row = lax.rsqrt(totals[0:2, :] / D + EPSILON)
    scale_row = inverse_row * inverse_row * inverse_row / D * totals[2:4, :]
    turned = jnp.concatenate([inverse_row, scale_row, jnp.zeros((124, 128), F32)], axis=0).T
    inverse = jnp.concatenate([turned[:, 0:1], turned[:, 1:2]], axis=0)
    scale = jnp.concatenate([turned[:, 2:3], turned[:, 3:4]], axis=0)
    hidden = hidden_buf[...]
    token_grad = (inverse * gain * sums[0:TOKENS, :] - hidden * scale).astype(BF16)
    grad_pair[0] = token_grad
    grad_copy = remote(grad_pair.at[0], grad_pair.at[1], pair_send, pair_recv, partner)
    grad_copy.start()
    normed = (hidden * inverse * gain).astype(BF16)

    def spread_rows(grads, side):
        for j in range(4):
            wide[j, pl.ds(j, TOKENS, stride=4), :] = grads

        def narrow(b, carry):
            here = pl.ds(pl.multiple_of(b * 128, 128), 128)
            for j in range(4):
                spread[side, here, j * COLS : (j + 1) * COLS] = wide[j, here, :].astype(BF16)
            return carry

        lax.fori_loop(0, ROWS // 128, narrow, 0)

    offsets = ((4, 0), (3, 5), (2, 6), (1, 7))
    part = PIECE // 4
    ways = ((0, 1), (1, -1))

    def group_dot(group, side):
        near, far = ((x + offset) % RING for offset in offsets[group])
        left = spread[side, :, pl.ds(pl.multiple_of((near // 2) * COLS, COLS), COLS)]
        right = spread[side, :, pl.ds(pl.multiple_of((far // 2) * COLS, COLS), COLS)]
        both = jnp.concatenate([left, right], axis=1)
        if side == 0:
            first = pl.multiple_of((near % 2) * (2 * PIECE) + core * PIECE, 64)
            return dot(rows_t[pl.ds(first, PIECE), :], both)
        return dot(rows_p[pl.ds(pl.multiple_of((near % 2) * PIECE, 64), PIECE), :], both)

    def reach(way, half):
        return 4 if way == half else 3

    def chain(way, sign, half, chunk, step):
        return remote(
            chain_out.at[way, half, chunk, step],
            chain_in.at[way, half, chunk, step],
            chain_send.at[way, half, chunk, step],
            chain_recv.at[way, half, chunk, step],
            {"dp": 2 * ((x + RING + sign) % RING) + core},
        )

    places = {offset: (g, i) for g, two in enumerate(offsets) for i, offset in enumerate(two)}

    def kept_block(offset, half, chunk):
        group, side = places[offset % RING]
        first = (2 * half + chunk) * part
        return kept[group, first : first + part, side * COLS : (side + 1) * COLS]

    def link(long, step):
        for chunk in range(2):
            for way, sign in ways:
                half = way if long else 1 - way
                far = reach(way, half)
                value = kept_block(sign * (far - step), half, chunk)
                if step:
                    chain(way, sign, half, chunk, step - 1).wait_recv()
                    value = value + chain_in[way, half, chunk, step - 1].astype(F32)
                chain_out[way, half, chunk, step] = value.astype(BF16)
                chain(way, sign, half, chunk, step).start()

    norm_out[...] = dot_first(pick[...], normed).astype(BF16)
    exchange(norm_out, norm_in, norm_send, norm_recv)
    spread_rows(token_grad.astype(F32), 0)
    for group in range(4):
        kept[group] = group_dot(group, 0)
    grad_copy.wait_recv()
    spread_rows(grad_pair[1].astype(F32), 1)
    remote(rows_p, rows_p, turn_send, turn_recv, partner).wait_recv()
    for group in range(4):
        kept[group] = kept[group] + group_dot(group, 1)
        if group == 0:
            link(True, 0)
        if group == 1:
            link(False, 0)
    for step in range(1, 4):
        link(True, step)
        if step < 3:
            link(False, step)
        if step == 2:
            exchanged(norm_out, norm_in, norm_send, norm_recv)
            home = pos_key[...] == iota((ROUTED, TOKENS), 1).astype(F32)
            home = home.astype(F32).astype(BF16)
            normed_out[...] = dot_first(home, norm_in[...]).astype(BF16)

    for half in (1, 0):
        for chunk in range(2):
            value = kept_block(0, half, chunk)
            for way, sign in ways[:: -1 if half else 1]:
                last = reach(way, half) - 1
                chain(way, sign, half, chunk, last).wait_recv()
                value = value + chain_in[way, half, chunk, last].astype(F32)
            first = (2 * half + chunk) * part
            grad_out[first : first + part, :] = value

    for half in range(2):
        sent = rows.at[pl.ds(0, (MEMBERS - 1) * SLOTS), pl.ds(half * HALF, HALF)]
        remote(
            sent, sent, gather_send.at[half], gather_recv.at[half, 0], {"rep": (y + 1) % RING}
        ).wait_send()
    sent = pl.ds(0, (GROUPS - 1) * BLOCK)
    for out_buf, send, recv in ((sum_out, sum_send, sum_recv), (norm_out, norm_send, norm_recv)):
        remote(
            out_buf.at[sent, :], out_buf.at[sent, :], send, recv.at[0], {"dp": (d + 1) % GROUPS}
        ).wait_send()
    sent = pl.ds(0, RING - 1)
    for slot, in_buf, recv in ((0, z_in, z_recv), (1, y_in, y_recv)):
        remote(
            in_buf.at[sent], in_buf.at[sent], stat_send.at[slot], recv.at[0], {"mp": (z + 1) % RING}
        ).wait_send()
    grad_copy.wait_send()
    remote(rows_p, rows_p, turn_send, turn_recv, partner).wait_send()
    for half in range(2):
        for chunk in range(2):
            for way, sign in ways:
                for step in range(reach(way, half)):
                    chain(way, sign, half, chunk, step).wait_send()


def on_device(
    query_rows,
    key_rows,
    value_rows,
    residual,
    out_proj,
    merge_gain,
    merger_proj,
    model_gain,
    image_grid,
    image_group,
    rollout_image,
    cotangent,
):
    hbm = pl.BlockSpec(memory_space=pltpu.HBM)
    vmem = pl.BlockSpec(memory_space=pltpu.VMEM)
    dma = pltpu.SemaphoreType.DMA
    part = PIECE // 4
    return pl.pallas_call(
        kernel,
        out_shape=(
            jax.ShapeDtypeStruct((TOKENS, COLS), BF16),
            jax.ShapeDtypeStruct((PIECE, COLS), F32),
        ),
        in_specs=[hbm] * 12,
        out_specs=(vmem, vmem),
        scratch_shapes=[
            pltpu.VMEM((10, 128), F32),
            pltpu.VMEM((1, COLS), F32),
            pltpu.VMEM((2, GROUPS * MEMBERS), jnp.int32),
            pltpu.VMEM((8, 128), jnp.int32),
            pltpu.VMEM((8, 128), jnp.int32),
            pltpu.VMEM((SLOTS, DV), BF16),
            pltpu.VMEM((SLOTS, DV), BF16),
            pltpu.VMEM((SLOTS, DV), BF16),
            pltpu.VMEM((SLOTS, DV), BF16),
            pltpu.VMEM((DV, DV), BF16),
            pltpu.VMEM((DV, 4 * COLS), BF16),
            pltpu.VMEM((4096, COLS), BF16),
            pltpu.VMEM((SLOTS, DV), BF16),
            pltpu.VMEM((ROWS, DV), BF16),
            pltpu.VMEM((DV, ROWS), BF16),
            pltpu.VMEM((4, ROWS, COLS), F32),
            pltpu.VMEM((2, ROWS, 4 * COLS), BF16),
            pltpu.VMEM((ROUTED, 1), F32),
            pltpu.VMEM((ROUTED, 1), F32),
            pltpu.VMEM((8, 512), F32),
            pltpu.VMEM((ROUTED, COLS), F32),
            pltpu.VMEM((ROUTED, COLS), BF16),
            pltpu.VMEM((ROUTED, COLS), BF16),
            pltpu.VMEM((TOKENS, ROUTED), BF16),
            pltpu.VMEM((TOKENS, COLS), F32),
            pltpu.VMEM((2, 4, 128), F32),
            pltpu.VMEM((RING, 4, 128), F32),
            pltpu.VMEM((RING, 4, 128), F32),
            pltpu.VMEM((ROUTED, COLS), BF16),
            pltpu.VMEM((ROUTED, COLS), BF16),
            pltpu.VMEM((4, PIECE, 2 * COLS), F32),
            pltpu.VMEM((2 * PIECE, ROWS), BF16),
            pltpu.VMEM((2, TOKENS, COLS), BF16),
            pltpu.VMEM((2, 2, 2, 4, part, COLS), BF16),
            pltpu.VMEM((2, 2, 2, 4, part, COLS), BF16),
            dma((15,)),
            dma((2,)),
            dma((2, MEMBERS)),
            dma,
            dma((GROUPS,)),
            dma((2,)),
            dma((RING,)),
            dma((RING,)),
            dma,
            dma((GROUPS,)),
            dma,
            dma,
            dma,
            dma,
            dma((2, 2, 2, 4)),
            dma((2, 2, 2, 4)),
        ],
        compiler_params=pltpu.CompilerParams(collective_id=0, has_side_effects=True, vmem_limit_bytes=36 << 20),
        name="merge_step",
    )(*(pltpu.with_memory_space_constraint(value, pltpu.HBM) for value in (
        query_rows,
        key_rows,
        value_rows,
        residual,
        out_proj,
        merge_gain.reshape(10, 128),
        merger_proj,
        model_gain.reshape(1, COLS),
        image_grid.T,
        image_group.reshape(8, 128),
        rollout_image.reshape(8, 128),
        cotangent,
    )))


def solution(mesh):
    return jax.shard_map(
        on_device,
        mesh=mesh,
        in_specs=(
            P(("dp", "mp", "rep"), None),
            P(("dp", "mp", "rep"), None),
            P(("dp", "mp", "rep"), None),
            P(("dp", "mp", "rep"), None),
            P(),
            P(),
            P(None, ("mp", "rep")),
            P(("mp", "rep")),
            P(),
            P(),
            P("dp"),
            P("dp", ("mp", "rep")),
        ),
        out_specs=(P("dp", ("mp", "rep")), P("dp", ("mp", "rep"))),
        check_vma=False,
    )
```

```python
import functools

import jax
import jax.numpy as jnp
from jax import lax
from jax.experimental import pallas as pl
from jax.experimental.pallas import tpu as pltpu
from jax.sharding import PartitionSpec as P

HEADS = 16
HEAD = 80
DV = 1280
D = 8192
EPSILON = 1e-06
RING = 8
GROUPS = 16
MEMBERS = 64
SLOTS = 16
ROWS = MEMBERS * SLOTS
TOKENS = MEMBERS * 4
HALF = DV // 2
COLS = 128
BLOCK = 32
ROUTED = GROUPS * BLOCK
PIECE = 320
MESH = pl.DeviceIdType.MESH
F32 = jnp.float32
BF16 = jnp.bfloat16


def iota(shape, dim):
    return lax.broadcasted_iota(jnp.int32, shape, dim)


def dot(a, b):
    return jnp.dot(a, b, preferred_element_type=F32)


def dot_first(a, b):
    return lax.dot_general(a, b, (((0,), (0,)), ((), ())), preferred_element_type=F32)


def remote(src, dst, send, recv, device):
    return pltpu.make_async_remote_copy(
        src_ref=src,
        dst_ref=dst,
        send_sem=send,
        recv_sem=recv,
        device_id=device,
        device_id_type=MESH,
    )


def kernel(
    q_hbm,
    k_hbm,
    v_hbm,
    res_hbm,
    wo_hbm,
    merge_gain_hbm,
    w_hbm,
    gain_hbm,
    grid_hbm,
    group_hbm,
    roll_hbm,
    cot_hbm,
    normed_out,
    grad_out,
    merge_gain_ref,
    gain_ref,
    grid_ref,
    group_ref,
    roll_ref,
    q_buf,
    k_buf,
    v_buf,
    res_buf,
    wo_buf,
    w_buf,
    cot_buf,
    own_buf,
    rows,
    rows_t,
    wide,
    spread,
    row_key,
    pos_key,
    col_key,
    sums,
    sum_out,
    sum_in,
    pick,
    hidden_buf,
    packet,
    z_in,
    y_in,
    norm_out,
    norm_in,
    kept,
    rows_p,
    grad_pair,
    chain_out,
    chain_in,
    load_sem,
    gather_send,
    gather_recv,
    sum_send,
    sum_recv,
    stat_send,
    z_recv,
    y_recv,
    norm_send,
    norm_recv,
    turn_send,
    turn_recv,
    pair_send,
    pair_recv,
    chain_send,
    chain_recv,
):
    d = lax.axis_index("dp")
    z = lax.axis_index("mp")
    y = lax.axis_index("rep")
    x = d // 2
    core = d % 2

    barrier = pltpu.get_barrier_semaphore()

    def greet(axis, me, size):
        def step(i, carry):
            pl.semaphore_signal(
                barrier, inc=1, device_id={axis: (me + i) % size}, device_id_type=MESH
            )
            return carry

        lax.fori_loop(1, size, step, 0)

    greet("mp", z, RING)
    greet("rep", y, RING)
    greet("dp", d, GROUPS)

    smalls = [
        pltpu.make_async_copy(grid_hbm, grid_ref, load_sem.at[10]),
        pltpu.make_async_copy(merge_gain_hbm, merge_gain_ref, load_sem.at[11]),
        pltpu.make_async_copy(group_hbm, group_ref, load_sem.at[12]),
        pltpu.make_async_copy(roll_hbm, roll_ref, load_sem.at[13]),
        pltpu.make_async_copy(gain_hbm, gain_ref, load_sem.at[14]),
    ]
    loads = [
        pltpu.make_async_copy(q_hbm, q_buf, load_sem.at[0]),
        pltpu.make_async_copy(k_hbm, k_buf, load_sem.at[1]),
        pltpu.make_async_copy(v_hbm, v_buf, load_sem.at[2]),
        pltpu.make_async_copy(res_hbm, res_buf, load_sem.at[3]),
        pltpu.make_async_copy(wo_hbm, wo_buf, load_sem.at[4]),
        pltpu.make_async_copy(cot_hbm, cot_buf, load_sem.at[5]),
    ] + [
        pltpu.make_async_copy(
            w_hbm.at[pl.ds(j * DV, DV), :], w_buf.at[:, pl.ds(j * COLS, COLS)], load_sem.at[6 + j]
        )
        for j in range(4)
    ]
    smalls[0].start()
    for load in loads[:5] + smalls[1:] + loads[5:]:
        load.start()

    smalls[0].wait()
    factors = grid_ref[...]
    products = factors[0:1, :] * factors[1:2, :]
    counts = jnp.concatenate(
        [products[:, 128 * a : 128 * a + 128] for a in range(8)], axis=0
    ).astype(F32)
    sub8 = iota((8, 128), 0)
    lane8 = iota((8, 128), 1)
    own_image = d * MEMBERS + z * RING + y
    is_own = (sub8 == own_image // 128) & (lane8 == own_image % 128)
    own_count = jnp.sum(
        jnp.sum(jnp.where(is_own, counts, 0.0), axis=0, keepdims=True), axis=1, keepdims=True
    )
    own_valid = own_count * 4.0

    loads[0].wait()
    loads[1].wait()
    head_of_row = iota((256, DV), 0) // SLOTS
    feature = iota((256, DV), 1)
    in_head = (feature >= head_of_row * HEAD) & (feature < head_of_row * HEAD + HEAD)
    queries = jnp.concatenate([q_buf[...].astype(F32)] * HEADS, axis=0)
    queries = jnp.where(in_head, queries, 0.0).astype(BF16)
    scores = lax.dot_general(
        queries, k_buf[...], (((1,), (1,)), ((), ())), preferred_element_type=F32
    ) * HEAD ** (-0.5)
    key_slot = iota((256, SLOTS), 1).astype(F32)
    scores = jnp.where(key_slot < own_valid, scores, -1e30)
    top = jnp.max(scores, axis=1, keepdims=True)
    powers = jnp.exp(scores - top)
    weights = (powers / jnp.sum(powers, axis=1, keepdims=True)).astype(BF16)
    loads[2].wait()
    attended = jnp.where(in_head, dot(weights, v_buf[...]), 0.0)
    attended = jnp.sum(attended.reshape(HEADS, SLOTS, DV), axis=0).astype(BF16)
    loads[3].wait()
    loads[4].wait()
    mixed = res_buf[...].astype(F32) + dot(attended, wo_buf[...])
    inverse_rms = lax.rsqrt(jnp.sum(mixed * mixed, axis=1, keepdims=True) / DV + EPSILON)
    slot_valid = (iota((SLOTS, 1), 0).astype(F32) < own_valid).astype(F32)
    smalls[1].wait()
    merge_gain = jnp.concatenate([merge_gain_ref[i : i + 1, :] for i in range(10)], axis=1)
    own_buf[...] = (mixed * inverse_rms * merge_gain * slot_valid).astype(BF16)

    def image_rows(zz, yy):
        return pl.ds(pl.multiple_of((zz * RING + yy) * SLOTS, SLOTS), SLOTS)

    def half_of(half, zz, yy):
        return rows.at[image_rows(zz, yy), pl.ds(half * HALF, HALF)]

    pl.semaphore_wait(barrier, 2 * (RING - 1) + GROUPS - 1)

    def push(half, src, zz, yy, device):
        remote(
            src,
            half_of(half, zz, yy),
            gather_send.at[half],
            gather_recv.at[half, zz * RING + yy],
            device,
        ).start()

    def arrive(half, zz, yy):
        ref = half_of(half, zz, yy)
        remote(
            ref,
            ref,
            gather_send.at[half],
            gather_recv.at[half, zz * RING + yy],
            {"rep": (y + 1) % RING},
        ).wait_recv()

    up_y, down_y = {"rep": (y + 1) % RING}, {"rep": (y + RING - 1) % RING}
    up_z, down_z = {"mp": (z + 1) % RING}, {"mp": (z + RING - 1) % RING}
    own0 = own_buf.at[:, pl.ds(0, HALF)]
    own1 = own_buf.at[:, pl.ds(HALF, HALF)]

    def shift(o):
        return (1 - 2 * (o % 2)) * ((o + 1) // 2)

    push(0, own0, z, y, up_y)
    push(0, own0, z, y, down_y)
    push(1, own1, z, y, up_z)
    push(1, own1, z, y, down_z)

    def spread_own(o, carry):
        push(0, own0, z, y, {"mp": (z + RING + shift(o)) % RING})
        push(1, own1, z, y, {"rep": (y + RING + shift(o)) % RING})
        return carry

    lax.fori_loop(1, RING, spread_own, 0)
    rows[image_rows(z, y), :] = own_buf[...]

    partner = {"dp": 2 * x + 1 - core}

    def project(plane):
        here = pl.ds(pl.multiple_of(plane * 128, 128), 128)
        product = dot(rows[here, :], w_buf[...])
        for j in range(4):
            wide[j, here, :] = product[:, j * COLS : (j + 1) * COLS]

    def turn(half, plane):
        here = pl.ds(pl.multiple_of(plane * 128, 128), 128)
        features = slice(half * HALF, (half + 1) * HALF)
        rows_t[features, here] = rows[here, features].T
        first = pl.multiple_of(HALF * half + (1 - core) * PIECE, 64)
        remote(
            rows_t.at[pl.ds(first, PIECE), here],
            rows_p.at[pl.ds(half * PIECE, PIECE), here],
            turn_send,
            turn_recv,
            partner,
        ).start()

    for load in smalls[2:]:
        load.wait()
    groups = group_ref[...]
    arriving = groups == d
    arrived = arriving.astype(F32).astype(BF16)
    before = iota((128, 128), 0)
    after = iota((128, 128), 1)
    earlier = before < after
    rank_in_owner = dot(
        arrived, (earlier & (before // MEMBERS == after // MEMBERS)).astype(F32).astype(BF16)
    )
    rank_in_chunk = dot(arrived, earlier.astype(F32).astype(BF16))
    lower = (iota((8, 8), 0) > iota((8, 8), 1)).astype(F32).astype(BF16)
    chunk_start = jnp.sum(dot(lower, arrived), axis=1, keepdims=True)
    place = rank_in_chunk + chunk_start
    slot_in_chunk = jnp.where(
        arriving, (lane8 // MEMBERS).astype(F32) * 8.0 + rank_in_owner, -1.0
    )
    image_key = (sub8 * 128 + lane8).astype(F32) * 4.0
    slot_of_row = (iota((64, 128), 0) // 4).astype(F32)
    token_of_row = (iota((64, 1), 0) % 4).astype(F32)
    for a in range(8):
        match = slot_in_chunk[a : a + 1, :] == slot_of_row

        def total(value):
            return jnp.sum(jnp.where(match, value[a : a + 1, :], 0.0), axis=1, keepdims=True)

        found = total(counts)
        row_key[64 * a : 64 * a + 64, :] = jnp.where(
            token_of_row < found, total(image_key) + token_of_row, -1.0
        )
        pos_key[64 * a : 64 * a + 64, :] = jnp.where(
            found > 0.0, total(place) * 4.0 + token_of_row, -1.0
        )
    rollouts = roll_ref[...]
    widen = (iota((128, 512), 0) == iota((128, 512), 1) // 4).astype(F32).astype(BF16)
    high = dot((rollouts // 32).astype(F32).astype(BF16), widen)
    low = dot((rollouts % 32).astype(F32).astype(BF16), widen)
    col_key[...] = (high * 32.0 + low) * 4.0 + (iota((8, 512), 1) % 4).astype(F32)
    sums[...] = jnp.zeros_like(sums)
    loads[5].wait()

    def add_chunk(a):
        chosen = (row_key[...] == col_key[pl.ds(a, 1), :]).astype(F32).astype(BF16)
        part = cot_buf[pl.ds(pl.multiple_of(a * 512, 512), 512), :]
        sums[...] += dot(chosen, part)


    def first_axis(o):
        zz = (z + RING + shift(o)) % RING
        yy = (y + RING + shift(o)) % RING
        arrive(0, zz, y)
        push(0, half_of(0, zz, y), zz, y, up_y)
        push(0, half_of(0, zz, y), zz, y, down_y)
        arrive(1, z, yy)
        push(1, half_of(1, z, yy), z, yy, up_z)
        push(1, half_of(1, z, yy), z, yy, down_z)

    def first_axis_step(o, carry):
        first_axis(o)
        return carry

    lax.fori_loop(1, RING, first_axis_step, 0)

    def hop(h, o, up, down):
        zz = (z + RING + shift(o)) % RING
        yy = (y + RING + shift(o)) % RING
        below, above = (y + RING - h) % RING, (y + h) % RING
        arrive(0, zz, below)
        if up:
            push(0, half_of(0, zz, below), zz, below, up_y)
        arrive(0, zz, above)
        if down:
            push(0, half_of(0, zz, above), zz, above, down_y)
        below, above = (z + RING - h) % RING, (z + h) % RING
        arrive(1, below, yy)
        if up:
            push(1, half_of(1, below, yy), below, yy, up_z)
        arrive(1, above, yy)
        if down:
            push(1, half_of(1, above, yy), above, yy, down_z)

    def first_hop(i, carry):
        hop(1, 2 * i, True, True)
        hop(1, 2 * i + 1, True, True)
        add_chunk(i)
        return carry

    turn(1, z)
    lax.fori_loop(0, RING // 2, first_hop, 0)
    turn(1, (z + 1) % RING)
    turn(1, (z + 7) % RING)

    def second_hop(i, carry):
        hop(2, 2 * i, True, True)
        hop(2, 2 * i + 1, True, True)
        add_chunk(i + 4)
        return carry

    lax.fori_loop(0, RING // 2, second_hop, 0)
    sum_out[...] = sums[...].astype(BF16)

    def routed(buf, peer):
        return buf.at[pl.ds(pl.multiple_of(peer * BLOCK, BLOCK), BLOCK), :]

    def exchange(out_buf, in_buf, send, recv):
        def step(i, carry):
            peer = (d + i) % GROUPS
            remote(
                routed(out_buf, peer), routed(in_buf, d), send, recv.at[d], {"dp": peer}
            ).start()
            return carry

        lax.fori_loop(1, GROUPS, step, 0)
        here = pl.ds(pl.multiple_of(d * BLOCK, BLOCK), BLOCK)
        in_buf[here, :] = out_buf[here, :]

    def exchanged(out_buf, in_buf, send, recv):
        def step(i, carry):
            peer = (d + i) % GROUPS
            remote(
                routed(out_buf, peer), routed(in_buf, peer), send, recv.at[peer], {"dp": peer}
            ).wait_recv()
            return carry

        lax.fori_loop(1, GROUPS, step, 0)

    exchange(sum_out, sum_in, sum_send, sum_recv)

    turn(1, (z + 2) % RING)
    turn(1, (z + 6) % RING)

    def third_hop(i, carry):
        hop(3, 2 * i, True, False)
        hop(3, 2 * i + 1, False, True)
        return carry

    lax.fori_loop(0, RING // 2, third_hop, 0)
    turn(1, (z + 3) % RING)
    turn(1, (z + 5) % RING)

    own_half = (d % 2) * MEMBERS
    own_dest = jnp.sum(
        jnp.where(sub8 == d // 2, groups.astype(F32), 0.0), axis=0, keepdims=True
    )
    lane = iota((TOKENS, 128), 1)
    own_lane = own_half + iota((TOKENS, 128), 0) // 4
    dest = jnp.sum(jnp.where(lane == own_lane, own_dest, 0.0), axis=1, keepdims=True)
    same = (own_dest == dest) & (lane >= own_half) & (lane < own_lane)
    rank = jnp.sum(jnp.where(same, 1.0, 0.0), axis=1, keepdims=True)
    token = (iota((TOKENS, 1), 0) % 4).astype(F32)
    slot_row = dest * BLOCK + rank * 4.0 + token
    pick[...] = (slot_row == iota((TOKENS, ROUTED), 1).astype(F32)).astype(F32).astype(BF16)
    for load in loads[6:]:
        load.wait()

    def last_hop(o, carry):
        zz = (z + RING + shift(o)) % RING
        arrive(0, zz, (y + 4) % RING)
        arrive(1, (z + 4) % RING, (y + RING + shift(o)) % RING)
        project(zz)
        return carry

    lax.fori_loop(0, RING, last_hop, 0)
    outputs = wide[0, pl.ds(0, TOKENS, stride=4), :]
    for j in range(1, 4):
        outputs += wide[j, pl.ds(j, TOKENS, stride=4), :]
    hidden = outputs.astype(BF16).astype(F32)
    hidden_buf[...] = hidden
    gain = gain_ref[...]
    exchanged(sum_out, sum_in, sum_send, sum_recv)
    summed = dot(pick[...], sum_in[...])
    sums[0:TOKENS, :] = summed
    squares = jnp.sum((hidden * hidden).T, axis=0, keepdims=True)
    inner = jnp.sum((summed * gain * hidden).T, axis=0, keepdims=True)
    packet[0] = jnp.concatenate(
        [
            squares[:, 0:128],
            squares[:, 128:256],
            inner[:, 0:128],
            inner[:, 128:256],
        ],
        axis=0,
    )

    def share(slot, axis, me, in_buf, recv):
        def step(i, carry):
            remote(
                packet.at[slot],
                in_buf.at[me],
                stat_send.at[slot],
                recv.at[me],
                {axis: (me + i) % RING},
            ).start()
            return carry

        lax.fori_loop(1, RING, step, 0)
        in_buf[me] = packet[slot]

    def shared(slot, axis, me, in_buf, recv):
        def step(i, carry):
            peer = (me + i) % RING
            remote(
                packet.at[slot], in_buf.at[peer], stat_send.at[slot], recv.at[peer], {axis: peer}
            ).wait_recv()
            return carry

        lax.fori_loop(1, RING, step, 0)
        return jnp.sum(in_buf[...], axis=0)

    def turn_first(plane, carry):
        turn(0, plane)
        return carry

    share(0, "mp", z, z_in, z_recv)
    lax.fori_loop(0, RING, turn_first, 0)
    turn(1, (z + 4) % RING)
    packet[1] = shared(0, "mp", z, z_in, z_recv)
    share(1, "rep", y, y_in, y_recv)
    wide[...] = jnp.zeros_like(wide)
    totals = shared(1, "rep", y, y_in, y_recv)

    inverse_row = lax.rsqrt(totals[0:2, :] / D + EPSILON)
    scale_row = inverse_row * inverse_row * inverse_row / D * totals[2:4, :]
    turned = jnp.concatenate([inverse_row, scale_row, jnp.zeros((124, 128), F32)], axis=0).T
    inverse = jnp.concatenate([turned[:, 0:1], turned[:, 1:2]], axis=0)
    scale = jnp.concatenate([turned[:, 2:3], turned[:, 3:4]], axis=0)
    hidden = hidden_buf[...]
    token_grad = (inverse * gain * sums[0:TOKENS, :] - hidden * scale).astype(BF16)
    grad_pair[0] = token_grad
    grad_copy = remote(grad_pair.at[0], grad_pair.at[1], pair_send, pair_recv, partner)

    def send_grad(i, carry):
        here = pl.ds(pl.multiple_of(i * 32, 32), 32)
        remote(
            grad_pair.at[0, here], grad_pair.at[1, here], pair_send, pair_recv, partner
        ).start()
        return carry

    lax.fori_loop(0, TOKENS // 32, send_grad, 0)
    normed = (hidden * inverse * gain).astype(BF16)

    def spread_rows(grads, side):
        for j in range(4):
            wide[j, pl.ds(j, TOKENS, stride=4), :] = grads

        def narrow(b, carry):
            here = pl.ds(pl.multiple_of(b * 128, 128), 128)
            for j in range(4):
                spread[side, here, j * COLS : (j + 1) * COLS] = wide[j, here, :].astype(BF16)
            return carry

        lax.fori_loop(0, ROWS // 128, narrow, 0)

    offsets = ((4, 0), (3, 5), (2, 6), (1, 7))
    part = PIECE // 4
    ways = ((0, 1), (1, -1))

    def group_dot(group, side):
        near, far = ((x + offset) % RING for offset in offsets[group])
        left = spread[side, :, pl.ds(pl.multiple_of((near // 2) * COLS, COLS), COLS)]
        right = spread[side, :, pl.ds(pl.multiple_of((far // 2) * COLS, COLS), COLS)]
        both = jnp.concatenate([left, right], axis=1)
        if side == 0:
            first = pl.multiple_of((near % 2) * (2 * PIECE) + core * PIECE, 64)
            return dot(rows_t[pl.ds(first, PIECE), :], both)
        return dot(rows_p[pl.ds(pl.multiple_of((near % 2) * PIECE, 64), PIECE), :], both)

    def reach(way, half):
        return 4 if way == half else 3

    def chain(way, sign, half, chunk, step):
        return remote(
            chain_out.at[way, half, chunk, step],
            chain_in.at[way, half, chunk, step],
            chain_send.at[way, half, chunk, step],
            chain_recv.at[way, half, chunk, step],
            {"dp": 2 * ((x + RING + sign) % RING) + core},
        )

    places = {offset: (g, i) for g, two in enumerate(offsets) for i, offset in enumerate(two)}

    def kept_block(offset, half, chunk):
        group, side = places[offset % RING]
        first = (2 * half + chunk) * part
        return kept[group, first : first + part, side * COLS : (side + 1) * COLS]

    def link(long, step):
        for chunk in range(2):
            for way, sign in ways:
                half = way if long else 1 - way
                far = reach(way, half)
                value = kept_block(sign * (far - step), half, chunk)
                if step:
                    chain(way, sign, half, chunk, step - 1).wait_recv()
                    value = value + chain_in[way, half, chunk, step - 1].astype(F32)
                chain_out[way, half, chunk, step] = value.astype(BF16)
                chain(way, sign, half, chunk, step).start()

    norm_out[...] = dot_first(pick[...], normed).astype(BF16)
    exchange(norm_out, norm_in, norm_send, norm_recv)
    spread_rows(token_grad.astype(F32), 0)
    for group in range(4):
        kept[group] = group_dot(group, 0)
    grad_copy.wait_recv()
    spread_rows(grad_pair[1].astype(F32), 1)
    remote(rows_p, rows_p, turn_send, turn_recv, partner).wait_recv()
    for group in range(4):
        kept[group] = kept[group] + group_dot(group, 1)
        if group == 0:
            link(True, 0)
        if group == 1:
            link(False, 0)
    for step in range(1, 4):
        link(True, step)
        if step < 3:
            link(False, step)
        if step == 3:
            exchanged(norm_out, norm_in, norm_send, norm_recv)
            home = pos_key[...] == iota((ROUTED, TOKENS), 1).astype(F32)
            home = home.astype(F32).astype(BF16)
            normed_out[...] = dot_first(home, norm_in[...]).astype(BF16)

    for half in (1, 0):
        for chunk in range(2):
            value = kept_block(0, half, chunk)
            for way, sign in ways[:: -1 if half else 1]:
                last = reach(way, half) - 1
                chain(way, sign, half, chunk, last).wait_recv()
                value = value + chain_in[way, half, chunk, last].astype(F32)
            first = (2 * half + chunk) * part
            grad_out[first : first + part, :] = value

    for half in range(2):
        sent = rows.at[pl.ds(0, (MEMBERS - 1) * SLOTS), pl.ds(half * HALF, HALF)]
        remote(
            sent, sent, gather_send.at[half], gather_recv.at[half, 0], {"rep": (y + 1) % RING}
        ).wait_send()
    sent = pl.ds(0, (GROUPS - 1) * BLOCK)
    for out_buf, send, recv in ((sum_out, sum_send, sum_recv), (norm_out, norm_send, norm_recv)):
        remote(
            out_buf.at[sent, :], out_buf.at[sent, :], send, recv.at[0], {"dp": (d + 1) % GROUPS}
        ).wait_send()
    sent = pl.ds(0, RING - 1)
    for slot, in_buf, recv in ((0, z_in, z_recv), (1, y_in, y_recv)):
        remote(
            in_buf.at[sent], in_buf.at[sent], stat_send.at[slot], recv.at[0], {"mp": (z + 1) % RING}
        ).wait_send()
    grad_copy.wait_send()
    remote(rows_p, rows_p, turn_send, turn_recv, partner).wait_send()
    for half in range(2):
        for chunk in range(2):
            for way, sign in ways:
                for step in range(reach(way, half)):
                    chain(way, sign, half, chunk, step).wait_send()


def on_device(
    query_rows,
    key_rows,
    value_rows,
    residual,
    out_proj,
    merge_gain,
    merger_proj,
    model_gain,
    image_grid,
    image_group,
    rollout_image,
    cotangent,
):
    hbm = pl.BlockSpec(memory_space=pltpu.HBM)
    vmem = pl.BlockSpec(memory_space=pltpu.VMEM)
    dma = pltpu.SemaphoreType.DMA
    part = PIECE // 4
    return pl.pallas_call(
        kernel,
        out_shape=(
            jax.ShapeDtypeStruct((TOKENS, COLS), BF16),
            jax.ShapeDtypeStruct((PIECE, COLS), F32),
        ),
        in_specs=[hbm] * 12,
        out_specs=(vmem, vmem),
        scratch_shapes=[
            pltpu.VMEM((10, 128), F32),
            pltpu.VMEM((1, COLS), F32),
            pltpu.VMEM((2, GROUPS * MEMBERS), jnp.int32),
            pltpu.VMEM((8, 128), jnp.int32),
            pltpu.VMEM((8, 128), jnp.int32),
            pltpu.VMEM((SLOTS, DV), BF16),
            pltpu.VMEM((SLOTS, DV), BF16),
            pltpu.VMEM((SLOTS, DV), BF16),
            pltpu.VMEM((SLOTS, DV), BF16),
            pltpu.VMEM((DV, DV), BF16),
            pltpu.VMEM((DV, 4 * COLS), BF16),
            pltpu.VMEM((4096, COLS), BF16),
            pltpu.VMEM((SLOTS, DV), BF16),
            pltpu.VMEM((ROWS, DV), BF16),
            pltpu.VMEM((DV, ROWS), BF16),
            pltpu.VMEM((4, ROWS, COLS), F32),
            pltpu.VMEM((2, ROWS, 4 * COLS), BF16),
            pltpu.VMEM((ROUTED, 1), F32),
            pltpu.VMEM((ROUTED, 1), F32),
            pltpu.VMEM((8, 512), F32),
            pltpu.VMEM((ROUTED, COLS), F32),
            pltpu.VMEM((ROUTED, COLS), BF16),
            pltpu.VMEM((ROUTED, COLS), BF16),
            pltpu.VMEM((TOKENS, ROUTED), BF16),
            pltpu.VMEM((TOKENS, COLS), F32),
            pltpu.VMEM((2, 4, 128), F32),
            pltpu.VMEM((RING, 4, 128), F32),
            pltpu.VMEM((RING, 4, 128), F32),
            pltpu.VMEM((ROUTED, COLS), BF16),
            pltpu.VMEM((ROUTED, COLS), BF16),
            pltpu.VMEM((4, PIECE, 2 * COLS), F32),
            pltpu.VMEM((2 * PIECE, ROWS), BF16),
            pltpu.VMEM((2, TOKENS, COLS), BF16),
            pltpu.VMEM((2, 2, 2, 4, part, COLS), BF16),
            pltpu.VMEM((2, 2, 2, 4, part, COLS), BF16),
            dma((15,)),
            dma((2,)),
            dma((2, MEMBERS)),
            dma,
            dma((GROUPS,)),
            dma((2,)),
            dma((RING,)),
            dma((RING,)),
            dma,
            dma((GROUPS,)),
            dma,
            dma,
            dma,
            dma,
            dma((2, 2, 2, 4)),
            dma((2, 2, 2, 4)),
        ],
        compiler_params=pltpu.CompilerParams(collective_id=0, has_side_effects=True, vmem_limit_bytes=36 << 20),
        name="merge_step",
    )(*(pltpu.with_memory_space_constraint(value, pltpu.HBM) for value in (
        query_rows,
        key_rows,
        value_rows,
        residual,
        out_proj,
        merge_gain.reshape(10, 128),
        merger_proj,
        model_gain.reshape(1, COLS),
        image_grid.T,
        image_group.reshape(8, 128),
        rollout_image.reshape(8, 128),
        cotangent,
    )))


def solution(mesh):
    return jax.shard_map(
        on_device,
        mesh=mesh,
        in_specs=(
            P(("dp", "mp", "rep"), None),
            P(("dp", "mp", "rep"), None),
            P(("dp", "mp", "rep"), None),
            P(("dp", "mp", "rep"), None),
            P(),
            P(),
            P(None, ("mp", "rep")),
            P(("mp", "rep")),
            P(),
            P(),
            P("dp"),
            P("dp", ("mp", "rep")),
        ),
        out_specs=(P("dp", ("mp", "rep")), P("dp", ("mp", "rep"))),
        check_vma=False,
    )
```
